256 devices in a mesh: seq: 32 (over x, z_hi, core), tensor: 8 (over z_lo, y).
Axes of the slice: x: 4, y: 4, z: 8 (z_hi: 4, z_lo: 2; z = z_hi * 2 + z_lo), core: 2. Of those that a mesh axis runs over, the one named last changes fastest.
Arguments:
- keyval: bfloat16 [16384, 8192], P('seq', 'tensor'), may hold values from -6 to 6
- gating: bfloat16 [16384, 8192], P('seq', 'tensor'), may hold values from -6 to 6
- skip_gain: float32 [8192], P('tensor'), may hold values from -4 to 4
- filter_values: float32 [2, 64, 2, 32, 8192], P(None, None, None, 'seq', 'tensor'), may hold values from -12 to 12
- blocks: int32 [64, 64], P('tensor'), may hold values from 0 to 255, as said below
- out_weight: bfloat16 [8192, 8192], P('seq', 'tensor'), may hold values from -0.0625 to 0.0625
Outputs:
- mixed: bfloat16 [16384, 8192], P('seq', 'tensor')
The draws below stay inside these ranges and needn't reach their ends.
Inputs may be any that keep to these rules, and one draw needn't show every extreme that they name: Each row names 64 different blocks.
All inputs are finite; a program needn't handle non-finite values.
Results may differ from the reference program's by a relative error of at most 0.0063.
Values may be sent and summed in bfloat16 or wider, within the bound.
A program may use at most 128 MiB of HBM per device.

```python
import math
import jax
import jax.numpy as jnp
from jax import lax

D = 8192
GROUP = 128
BLOCK = 64
TOK_DEV = 512
TOKENS = 16384
NBLK = 256
KEEP = 64
NGROUP = 64
N_SEQ = 32


def draw_blocks(key, part):
    row_keys = jax.random.split(jax.random.fold_in(key, 11), NGROUP)
    orders = jax.vmap(lambda row_key: jax.random.permutation(row_key, NBLK))(row_keys)
    chosen = orders[:, :KEEP].astype(jnp.int32)
    top_row = jax.random.randint(jax.random.fold_in(key, 12), (), 0, NGROUP)
    low_row = (top_row + 1) % NGROUP
    has_top = jnp.any(chosen == NBLK - 1, axis=1)
    has_low = jnp.any(chosen == 0, axis=1)
    row_index = jnp.arange(NGROUP, dtype=jnp.int32)
    force_top = jnp.logical_and(row_index == top_row, jnp.logical_not(has_top))
    force_low = jnp.logical_and(row_index == low_row, jnp.logical_not(has_low))
    first_column = jnp.where(force_top, NBLK - 1, jnp.where(force_low, 0, chosen[:, 0]))
    return chosen.at[:, 0].set(first_column.astype(jnp.int32))


def level_of(rng, extent, shards, least, top_value):
    factor_of, own = 1.0, jax.random.fold_in(rng, 6)
    for position, parts in shards:
        draws = jnp.exp(jax.random.uniform(jax.random.fold_in(own, position), (parts,), jnp.float32, least / len(shards), top_value / len(shards)))
        factor_of = factor_of * jnp.repeat(draws, extent[position] // parts).reshape([-1 if axis == position else 1 for axis in range(len(extent))])
    return factor_of


def centred(rng, dims, spread, bound, cuts=(), kind=jnp.bfloat16):
    loudness = level_of(rng, dims, cuts, -0.22, 0.18) if cuts else 1.0
    array = jax.random.normal(rng, dims, jnp.float32) * spread * loudness
    return jnp.minimum(jnp.maximum(array, -bound), bound).astype(kind)


def setup_inputs(seed: int = 0) -> dict:
    seeds = jax.random.split(jax.random.key(seed), 7)
    return {
        "keyval": centred(seeds[0], (TOKENS, D), 1.0, 6.0, ((0, 32), (1, 8))),
        "gating": centred(seeds[1], (TOKENS, D), 1.0, 6.0, ((0, 32), (1, 8))),
        "skip_gain": centred(seeds[2], (D,), 1.0, 4.0, ((0, 8),), jnp.float32),
        "filter_values": centred(seeds[3], (2, KEEP, BLOCK // N_SEQ, N_SEQ, D), 2.0, 12.0, ((3, 32), (4, 8)), jnp.float32),
        "blocks": draw_blocks(jax.random.fold_in(seeds[6], 71), 0),
        "out_weight": centred(seeds[5], (D, D), D ** -0.5, 0.0625, ((0, 32), (1, 8))),
    }


HIGHEST = lax.Precision.HIGHEST


def tables(first_index, second_index, length):
    phase = (first_index * second_index) % length
    angle = (2.0 * math.pi / length) * phase.astype(jnp.float32)
    return jnp.cos(angle), jnp.sin(angle)


def rounded(value):
    return lax.optimization_barrier(value.astype(jnp.bfloat16)).astype(jnp.float32)


def group_conv(keyval_group, block_list, filter_group):
    repeat = BLOCK // N_SEQ
    signal = keyval_group.astype(jnp.float32).reshape(N_SEQ, TOK_DEV, GROUP)
    cycle_index = jnp.arange(N_SEQ, dtype=jnp.int32)
    local_index = jnp.arange(TOK_DEV, dtype=jnp.int32)
    cosine_cycle, sine_cycle = tables(cycle_index[:, None], cycle_index[None, :], N_SEQ)
    first_real = jnp.einsum('pa,ajc->pjc', cosine_cycle, signal, precision=HIGHEST)
    first_imaginary = -jnp.einsum('pa,ajc->pjc', sine_cycle, signal, precision=HIGHEST)
    cosine_twist, sine_twist = tables(cycle_index[:, None], local_index[None, :], TOKENS)
    cosine_twist = cosine_twist[:, :, None]
    sine_twist = sine_twist[:, :, None]
    twist_real = rounded(first_real * cosine_twist + first_imaginary * sine_twist)
    twist_imaginary = rounded(first_imaginary * cosine_twist - first_real * sine_twist)
    kept_rows = (block_list[:, None] * repeat + jnp.arange(repeat, dtype=jnp.int32)[None, :]).reshape(-1)
    cosine_kept, sine_kept = tables(kept_rows[:, None], local_index[None, :], TOK_DEV)
    spectrum_real = (jnp.einsum('qj,pjc->pqc', cosine_kept, twist_real, precision=HIGHEST)
                     + jnp.einsum('qj,pjc->pqc', sine_kept, twist_imaginary, precision=HIGHEST))
    spectrum_imaginary = (jnp.einsum('qj,pjc->pqc', cosine_kept, twist_imaginary, precision=HIGHEST)
                          - jnp.einsum('qj,pjc->pqc', sine_kept, twist_real, precision=HIGHEST))
    filter_real = filter_group[0].reshape(KEEP * repeat, N_SEQ, GROUP).transpose(1, 0, 2)
    filter_imaginary = filter_group[1].reshape(KEEP * repeat, N_SEQ, GROUP).transpose(1, 0, 2)
    product_real = filter_real * spectrum_real - filter_imaginary * spectrum_imaginary
    product_imaginary = filter_real * spectrum_imaginary + filter_imaginary * spectrum_real
    back_real = (jnp.einsum('qj,pqc->pjc', cosine_kept, product_real, precision=HIGHEST)
                 - jnp.einsum('qj,pqc->pjc', sine_kept, product_imaginary, precision=HIGHEST))
    back_imaginary = (jnp.einsum('qj,pqc->pjc', sine_kept, product_real, precision=HIGHEST)
                      + jnp.einsum('qj,pqc->pjc', cosine_kept, product_imaginary, precision=HIGHEST))
    turned_real = rounded(back_real * cosine_twist - back_imaginary * sine_twist)
    turned_imaginary = rounded(back_real * sine_twist + back_imaginary * cosine_twist)
    convolved = (jnp.einsum('pa,pjc->ajc', cosine_cycle, turned_real, precision=HIGHEST)
                 - jnp.einsum('pa,pjc->ajc', sine_cycle, turned_imaginary, precision=HIGHEST)) / TOKENS
    return convolved.astype(jnp.bfloat16).reshape(TOKENS, GROUP)


def group_step(items):
    return group_conv(items[0], items[1], items[2])


def reference(keyval, gating, skip_gain, filter_values, blocks, out_weight):
    grouped = keyval.reshape(TOKENS, NGROUP, GROUP).transpose(1, 0, 2)
    filters = filter_values.reshape(2, KEEP, BLOCK // N_SEQ, N_SEQ, NGROUP, GROUP).transpose(4, 0, 1, 2, 3, 5)
    convolved = lax.map(group_step, (grouped, blocks, filters))
    convolved = convolved.transpose(1, 0, 2).reshape(TOKENS, D)
    hidden = (gating.astype(jnp.float32) * (convolved.astype(jnp.float32)
              + skip_gain[None, :] * keyval.astype(jnp.float32))).astype(jnp.bfloat16)
    return jnp.dot(hidden, out_weight, preferred_element_type=jnp.float32).astype(jnp.bfloat16)
```

```python
import functools
import math

import jax
import jax.numpy as jnp
from jax import lax
from jax.experimental import pallas as pl
from jax.experimental.pallas import tpu as pltpu
from jax.sharding import PartitionSpec as P

BLOCK = 64
SEQ = 32
OUTER = 8
INNER = 4
TOK = 512
QUARTER = 128
WIDTH = 1024
UNIT = 32
KEPT = 128
STEP = 16
ROWS = TOK // STEP
LENGTH = SEQ * TOK
F32 = jnp.float32
BF16 = jnp.bfloat16
MESH = pl.DeviceIdType.MESH


def iota(shape, axis):
    return lax.broadcasted_iota(jnp.int32, shape, axis)


def sine(x):
    s = x * x
    t = -1.0 / 39916800.0
    for c in (1.0 / 362880.0, -1.0 / 5040.0, 1.0 / 120.0, -1.0 / 6.0, 1.0):
        t = t * s + c
    return x * t


def cosine_of(phase):
    d = jnp.abs((phase & 511) - 256) - 128
    return sine(d.astype(F32) * (math.pi / 256.0))


def halves(v):
    hi = v.astype(BF16)
    return hi, (v - hi.astype(F32)).astype(BF16)


def dot(a, b):
    return jnp.dot(a, b, preferred_element_type=F32)


def turn(v, num, den, sign):
    re, im = v
    num = num % den
    if num == 0:
        return v
    if 4 * num == den:
        return (-im, re) if sign > 0 else (im, -re)
    c = math.cos(2 * math.pi * num / den)
    s = sign * math.sin(2 * math.pi * num / den)
    if 8 * num == den:
        h = c
        return (h * (re - im), h * (re + im)) if sign > 0 else (h * (re + im), h * (im - re))
    if 8 * num == 3 * den:
        h = -c
        return (-h * (re + im), h * (re - im)) if sign > 0 else (h * (im - re), -h * (re + im))
    return (re * c - im * s, re * s + im * c)


def transform(values, sign):
    n = len(values)
    if n == 1:
        return values
    even = transform(values[0::2], sign)
    odd = transform(values[1::2], sign)
    odd = [turn(o, k, n, sign) for k, o in enumerate(odd)]
    low = [(e[0] + o[0], e[1] + o[1]) for e, o in zip(even, odd)]
    high = [(e[0] - o[0], e[1] - o[1]) for e, o in zip(even, odd)]
    return low + high


def swap(parts, perm):
    u = dot(jnp.concatenate(parts, axis=1), perm[...]).astype(BF16)
    return [u[:, QUARTER * i : QUARTER * (i + 1)] for i in range(INNER)]


def kernel(
    tensor, kv, gate, skip, filt, kcol, krow, out,
    xs, xr, fs, fr, mh, ml, th, tl, dm, eh, el, perm, tw, rq, g, fst, fm, b, vh, vl, cs, cr, hid,
    xsend, xrecv, fsend, frecv, csend, crecv, gsend, grecv, local,
):
    me = lax.axis_index("seq")
    ten = lax.axis_index("tensor")
    zl, y = ten // 4, lax.rem(ten, 4)
    far = (1 - zl) * 4
    zp = far + y
    up, down = lax.rem(y + 1, 4), lax.rem(y + 3, 4)
    yp, ym = zl * 4 + up, zl * 4 + down

    barrier = pltpu.get_barrier_semaphore()

    @pl.loop(1, SEQ)
    def _(i):
        pl.semaphore_signal(
            barrier, inc=1, device_id={"seq": lax.rem(me + i, SEQ)}, device_id_type=MESH
        )

    if tensor:
        for t in (zp, yp, ym):
            pl.semaphore_signal(barrier, inc=1, device_id={"tensor": t}, device_id_type=MESH)

    @pl.loop(0, 8)
    def _(r):
        i = iota((64, 512), 0) + r * 64
        n = iota((64, 512), 1)
        same = ((i >> 7) == ((n >> 5) & 3)) & (((i >> 5) & 3) == (n >> 7)) & ((i & 31) == (n & 31))
        perm[pl.ds(pl.multiple_of(r * 64, 64), 64), :] = jnp.where(same, 1.0, 0.0).astype(BF16)

    def remote(src, dst, ss, rs, dev, axis="seq"):
        return pltpu.make_async_remote_copy(
            src_ref=src, dst_ref=dst, send_sem=ss, recv_sem=rs,
            device_id={axis: dev}, device_id_type=MESH,
        )

    def lanes(i):
        return pl.ds(pl.multiple_of(i * QUARTER, QUARTER), QUARTER)

    def deliver(dest, part, staged, landed, ss, rs):
        staged[dest] = part

        @pl.when(dest != me)
        def _():
            remote(staged.at[dest], landed.at[me], ss.at[dest], rs.at[me], dest).start()

        @pl.when(dest == me)
        def _():
            landed[me] = part

    def collect(landed, staged, ss, rs):
        @pl.loop(1, SEQ)
        def _(i):
            src = lax.rem(me + i, SEQ)
            remote(staged.at[src], landed.at[src], ss.at[src], rs.at[src], src).wait_recv()

    def settle(landed, staged, ss, rs):
        @pl.loop(1, SEQ)
        def _(i):
            src = lax.rem(me + i, SEQ)
            remote(staged.at[src], landed.at[src], ss.at[src], rs.at[src], src).wait_send()

    pl.semaphore_wait(barrier, SEQ - 1 + (3 if tensor else 0))

    @pl.loop(0, OUTER)
    def _(i):
        tile = lax.rem(me // INNER + i, OUTER)
        parts = [kv[QUARTER * k : QUARTER * (k + 1), lanes(tile)] for k in range(INNER)]
        for q, part in enumerate(swap(parts, perm)):
            deliver(tile * INNER + q, part, xs, xr, xsend, xrecv)

    @pl.loop(0, OUTER)
    def _(i):
        tile = lax.rem(me // INNER + i, OUTER)
        parts = []
        for k in range(INNER):
            pair = [
                filt[pl.ds(m * 1024 + 256 * k + tile, UNIT, stride=8), :].astype(BF16)
                for m in range(2)
            ]
            parts.append(jnp.concatenate(pair, axis=0))
        for q, part in enumerate(swap(parts, perm)):
            deliver(tile * INNER + q, part, fs, fr, fsend, frecv)

    @pl.loop(0, KEPT // STEP)
    def _(r):
        rows = pl.ds(pl.multiple_of(r * STEP, STEP), STEP)
        more = pl.ds(pl.multiple_of(r * STEP + KEPT, STEP), STEP)
        phase = kcol[rows, 0:1] * iota((STEP, TOK), 1)
        ch, cl = halves(cosine_of(phase))
        sn = cosine_of(phase - 128)
        sh, sl = halves(sn)
        nh, nl = halves(-sn)
        mh[rows, 0:TOK] = ch
        ml[rows, 0:TOK] = cl
        mh[rows, TOK:] = sh
        ml[rows, TOK:] = sl
        mh[more, 0:TOK] = nh
        ml[more, 0:TOK] = nl
        mh[more, TOK:] = ch
        ml[more, TOK:] = cl

    @pl.loop(0, TOK // 64)
    def _(r):
        rows = pl.ds(pl.multiple_of(r * 64, 64), 64)
        more = pl.ds(pl.multiple_of(r * 64 + TOK, 64), 64)
        phase = krow[0:1, :] * (iota((64, KEPT), 0) + r * 64)
        ch, cl = halves(cosine_of(phase))
        sn = cosine_of(phase - 128)
        sh, sl = halves(sn)
        nh, nl = halves(-sn)
        th[rows, 0:KEPT] = ch
        tl[rows, 0:KEPT] = cl
        th[rows, KEPT:] = nh
        tl[rows, KEPT:] = nl
        th[more, 0:KEPT] = sh
        tl[more, 0:KEPT] = sl
        th[more, KEPT:] = ch
        tl[more, KEPT:] = cl

    @pl.loop(0, OUTER)
    def _(a):
        i, n = iota((128, 256), 0), iota((128, 256), 1)
        phase = ((i >> 5) * 8 + a) * ((n >> 5) & 3) + 8 * (n >> 7)
        hi, lo = halves(jnp.where((i & 31) == (n & 31), cosine_of(phase * 16), 0.0))
        dm[a, 0:128, :] = hi
        dm[a, 128:256, :] = lo
        n, i = iota((256, 128), 0), iota((256, 128), 1)
        phase = ((i >> 5) * 8 + a) * ((n >> 5) & 3) + 8 * (n >> 7)
        hi, lo = halves(jnp.where((i & 31) == (n & 31), cosine_of(phase * 16), 0.0))
        eh[a] = hi
        el[a] = lo

    @pl.loop(0, ROWS)
    def _(r):
        rows = pl.ds(pl.multiple_of(r * STEP, STEP), STEP)
        j = iota((STEP, 128), 0) + r * STEP
        alpha = (j * (iota((STEP, 128), 1) >> 5)).astype(F32) * (2 * math.pi / LENGTH)
        beta = (j * INNER).astype(F32) * (2 * math.pi / LENGTH)
        tw[0, rows, :] = sine(math.pi / 2 - alpha)
        tw[1, rows, :] = sine(alpha)
        tw[2, rows, :] = sine(math.pi / 2 - beta)
        tw[3, rows, :] = sine(beta)

    collect(xr, xs, xsend, xrecv)

    @pl.loop(0, OUTER)
    def _(a):
        for k, part in enumerate(swap([xr[OUTER * l + a] for l in range(INNER)], perm)):
            rq[QUARTER * k : QUARTER * (k + 1), 0:128] = part
            rq[QUARTER * k : QUARTER * (k + 1), 128:256] = part
        g[a] = dot(rq[...], dm[a])

    def twists(rows):
        tc, ts = tw[0, rows, :], tw[1, rows, :]
        uc, us = tw[2, rows, :], tw[3, rows, :]
        found = []
        for p in range(OUTER):
            found.append((tc, ts))
            if p + 1 < OUTER:
                tc, ts = tc * uc - ts * us, ts * uc + tc * us
        return found

    @pl.loop(0, ROWS)
    def _(r):
        rows = pl.ds(pl.multiple_of(r * STEP, STEP), STEP)
        more = pl.ds(pl.multiple_of(r * STEP + TOK, STEP), STEP)
        first = transform([(g[a, rows, 0:128], g[a, rows, 128:256]) for a in range(OUTER)], -1)
        for p, ((re, im), (tc, ts)) in enumerate(zip(first, twists(rows))):
            cols = slice(128 * (p % 2), 128 * (p % 2) + 128)
            fst[p // 2, rows, cols] = (re * tc + im * ts).astype(BF16)
            fst[p // 2, more, cols] = (im * tc - re * ts).astype(BF16)

    collect(fr, fs, fsend, frecv)

    @pl.loop(0, OUTER // 2)
    def _(w):
        for half in range(2):
            p = 2 * w + half
            cols = slice(128 * half, 128 * half + 128)
            for k, part in enumerate(swap([fr[INNER * p + l] for l in range(INNER)], perm)):
                fm[0, UNIT * k : UNIT * (k + 1), cols] = part[0:UNIT]
                fm[1, UNIT * k : UNIT * (k + 1), cols] = part[UNIT:]
        spectrum = dot(mh[...], fst[w]) + dot(ml[...], fst[w])
        sr, si = spectrum[0:KEPT], spectrum[KEPT:]
        f_re, f_im = fm[0].astype(F32), fm[1].astype(F32)
        product = jnp.concatenate([f_re * sr - f_im * si, f_re * si + f_im * sr], axis=0)
        hi, lo = halves(product)
        b[w] = dot(th[...], hi) + dot(tl[...], hi) + dot(th[...], lo)

    @pl.loop(0, ROWS)
    def _(r):
        rows = pl.ds(pl.multiple_of(r * STEP, STEP), STEP)
        more = pl.ds(pl.multiple_of(r * STEP + TOK, STEP), STEP)
        turned = []
        for p, (tc, ts) in enumerate(twists(rows)):
            cols = slice(128 * (p % 2), 128 * (p % 2) + 128)
            re, im = b[p // 2, rows, cols], b[p // 2, more, cols]
            turned.append(
                (
                    (re * tc - im * ts).astype(BF16).astype(F32),
                    (re * ts + im * tc).astype(BF16).astype(F32),
                )
            )
        for a, (re, im) in enumerate(transform(turned, 1)):
            hi, lo = halves(re)
            vh[a, rows, 0:128] = hi
            vl[a, rows, 0:128] = lo
            hi, lo = halves(im)
            vh[a, rows, 128:256] = hi
            vl[a, rows, 128:256] = lo

    @pl.loop(0, OUTER)
    def _(i):
        a = lax.rem(lax.rem(me, OUTER) + i, OUTER)
        c = dot(vh[a], eh[a]) + dot(vl[a], eh[a]) + dot(vh[a], el[a])
        c = (c * (1.0 / LENGTH)).astype(BF16)
        for l, part in enumerate(swap([c[QUARTER * k : QUARTER * (k + 1)] for k in range(INNER)], perm)):
            deliver(OUTER * l + a, part, cs, cr, csend, crecv)

    collect(cr, cs, csend, crecv)

    @pl.loop(0, OUTER)
    def _(tile):
        for k, part in enumerate(swap([cr[INNER * tile + q] for q in range(INNER)], perm)):
            rows = slice(QUARTER * k, QUARTER * (k + 1))
            direct = skip[0:1, lanes(tile)] * kv[rows, lanes(tile)].astype(F32)
            hid[rows, lanes(tile)] = (
                gate[rows, lanes(tile)].astype(F32) * (part.astype(F32) + direct)
            ).astype(BF16)

    def cols(t):
        return pl.ds(pl.multiple_of(t * WIDTH, WIDTH), WIDTH)

    if tensor:
        top, bottom = slice(0, TOK // 2), slice(TOK // 2, TOK)

        def gather(index, src, rows, block, to):
            return remote(
                src, out.at[rows, cols(block)], gsend.at[index], grecv.at[index], to, "tensor"
            )

        every = slice(0, TOK)
        sends = [
            gather(0, hid, every, ten, zp),
            gather(1, hid, every, ten, yp),
            gather(2, hid, every, ten, ym),
        ]
        for c in sends:
            c.start()
        keep = pltpu.make_async_copy(hid, out.at[:, cols(ten)], local)
        keep.start()

        def arrived(index, rows, block):
            gather(index, out.at[rows, cols(block)], rows, block, zp).wait_recv()

        def relay(index, rows, block, to):
            c = gather(index, out.at[rows, cols(block)], rows, block, to)
            c.start()
            sends.append(c)

        arrived(0, every, zp)
        relay(3, every, zp, yp)
        relay(4, every, zp, ym)
        arrived(1, every, ym)
        relay(5, top, ym, yp)
        arrived(2, every, yp)
        relay(6, bottom, yp, ym)
        arrived(3, every, far + down)
        relay(7, top, far + down, yp)
        arrived(4, every, far + up)
        relay(8, bottom, far + up, ym)
        across = lax.rem(y + 2, 4)
        arrived(5, top, zl * 4 + across)
        arrived(6, bottom, zl * 4 + across)
        arrived(7, top, far + across)
        arrived(8, bottom, far + across)
        for c in sends:
            c.wait_send()
        keep.wait()
    else:
        pltpu.sync_copy(hid, out)

    settle(xr, xs, xsend, xrecv)
    settle(fr, fs, fsend, frecv)
    settle(cr, cs, csend, crecv)


def gathered_hidden(keyval, gating, skip_gain, filter_values, blocks, tensor):
    me = lax.axis_index("seq")
    groups = blocks.shape[0]
    group = me * groups // SEQ
    match = group == jnp.arange(groups, dtype=jnp.int32)
    kept = jnp.sum(jnp.where(match[:, None], blocks, 0), axis=0)
    kept = (kept[:, None] * 2 + jnp.arange(2, dtype=jnp.int32)[None, :]).reshape(KEPT)
    kcol = jnp.broadcast_to(kept[:, None], (KEPT, 128))
    krow = jnp.broadcast_to(kept[None, :], (8, KEPT))
    vmem = pl.BlockSpec(memory_space=pltpu.VMEM)
    dma = pltpu.SemaphoreType.DMA

    def buf(*shape, dtype=BF16):
        return pltpu.VMEM(shape, dtype)

    wide = WIDTH * (8 if tensor else 1)
    return pl.pallas_call(
        functools.partial(kernel, tensor),
        out_shape=jax.ShapeDtypeStruct((TOK, wide), BF16),
        in_specs=[vmem] * 6,
        out_specs=pl.BlockSpec(memory_space=pl.ANY),
        scratch_shapes=[
            buf(SEQ, 128, 128), buf(SEQ, 128, 128),
            buf(SEQ, 64, 128), buf(SEQ, 64, 128),
            buf(256, 1024), buf(256, 1024), buf(1024, 256), buf(1024, 256),
            buf(8, 256, 256), buf(8, 256, 128), buf(8, 256, 128), buf(512, 512),
            buf(4, 512, 128, dtype=F32), buf(512, 256), buf(8, 512, 256, dtype=F32),
            buf(4, 1024, 256), buf(2, 128, 256), buf(4, 1024, 256, dtype=F32),
            buf(8, 512, 256), buf(8, 512, 256),
            buf(SEQ, 128, 128), buf(SEQ, 128, 128), buf(TOK, WIDTH),
            dma((SEQ,)), dma((SEQ,)), dma((SEQ,)), dma((SEQ,)), dma((SEQ,)), dma((SEQ,)),
            dma((9,)), dma((9,)), dma,
        ],
        compiler_params=pltpu.CompilerParams(
            collective_id=0, has_side_effects=True, vmem_limit_bytes=50 * 2**20
        ),
        cost_estimate=pl.CostEstimate(flops=10**11, bytes_accessed=10**8, transcendentals=0),
    )(keyval, gating, skip_gain.reshape(1, WIDTH), filter_values.reshape(2048, 128), kcol, krow)


def body(keyval, gating, skip_gain, filter_values, blocks, out_weight):
    whole_weight = lax.all_gather(out_weight, "seq", axis=0, tiled=True)
    full_hidden = gathered_hidden(keyval, gating, skip_gain, filter_values, blocks, True)
    mixed = jnp.dot(full_hidden, whole_weight, preferred_element_type=F32)
    return mixed.astype(BF16)


def solution(mesh):
    placed = (
        P("seq", "tensor"),
        P("seq", "tensor"),
        P("tensor"),
        P(None, None, None, "seq", "tensor"),
        P("tensor", None),
        P("seq", "tensor"),
    )
    return jax.shard_map(
        body, mesh=mesh, in_specs=placed, out_specs=P("seq", "tensor"), check_vma=False
    )
```

```python
import math

import jax
import jax.numpy as jnp
from jax import lax
from jax.experimental import pallas as pl
from jax.experimental.pallas import tpu as pltpu
from jax.sharding import PartitionSpec as P

BLOCK = 64
SEQ = 32
OUTER = 8
INNER = 4
TOK = 512
QUARTER = 128
WIDTH = 1024
UNIT = 32
KEPT = 128
STEP = 16
ROWS = TOK // STEP
SPLIT = 288
LENGTH = SEQ * TOK
F32 = jnp.float32
BF16 = jnp.bfloat16
MESH = pl.DeviceIdType.MESH


def iota(shape, axis):
    return lax.broadcasted_iota(jnp.int32, shape, axis)


def sine(x):
    s = x * x
    t = -1.0 / 39916800.0
    for c in (1.0 / 362880.0, -1.0 / 5040.0, 1.0 / 120.0, -1.0 / 6.0, 1.0):
        t = t * s + c
    return x * t


def cosine_of(phase):
    d = jnp.abs((phase & 511) - 256) - 128
    return sine(d.astype(F32) * (math.pi / 256.0))


def halves(v):
    hi = v.astype(BF16)
    return hi, (v - hi.astype(F32)).astype(BF16)


def dot(a, b):
    return jnp.dot(a, b, preferred_element_type=F32)


def turn(v, num, den, sign):
    re, im = v
    num = num % den
    if num == 0:
        return v
    if 4 * num == den:
        return (-im, re) if sign > 0 else (im, -re)
    c = math.cos(2 * math.pi * num / den)
    s = sign * math.sin(2 * math.pi * num / den)
    if 8 * num == den:
        h = c
        return (h * (re - im), h * (re + im)) if sign > 0 else (h * (re + im), h * (im - re))
    if 8 * num == 3 * den:
        h = -c
        return (-h * (re + im), h * (re - im)) if sign > 0 else (h * (im - re), -h * (re + im))
    return (re * c - im * s, re * s + im * c)


def transform(values, sign):
    n = len(values)
    if n == 1:
        return values
    even = transform(values[0::2], sign)
    odd = transform(values[1::2], sign)
    odd = [turn(o, k, n, sign) for k, o in enumerate(odd)]
    low = [(e[0] + o[0], e[1] + o[1]) for e, o in zip(even, odd)]
    high = [(e[0] - o[0], e[1] - o[1]) for e, o in zip(even, odd)]
    return low + high


def swap(parts, perm):
    u = dot(jnp.concatenate(parts, axis=1), perm[...]).astype(BF16)
    return [u[:, QUARTER * i : QUARTER * (i + 1)] for i in range(INNER)]


def kernel(
    kv_in, gate_in, skip, filt_in, kcol, krow, weight_in, out,
    kv, gate, filt, xs, xr, fs, fr, mh, ml, th, tl, dm, eh, el, perm, tw, rq, g, fst, fm, vh, vl,
    cs, cr, gath, wv, acc,
    xsend, xrecv, fsend, frecv, csend, crecv, gsend, grecv, wsend, wrecv, local,
):
    me = lax.axis_index("seq")
    ten = lax.axis_index("tensor")
    zl, y = ten // 4, lax.rem(ten, 4)
    far, near = (1 - zl) * 4, zl * 4
    zp = far + y
    up, down, across = lax.rem(y + 1, 4), lax.rem(y + 3, 4), lax.rem(y + 2, 4)
    yp, ym = near + up, near + down
    core = lax.rem(me, 2)
    zh = lax.rem(me // 2, 4)
    x = me // 8
    first_core = core == 0

    loads = [
        pltpu.make_async_copy(kv_in, kv, local.at[0]),
        pltpu.make_async_copy(weight_in, wv.at[me], local.at[1]),
        pltpu.make_async_copy(filt_in, filt, local.at[2]),
        pltpu.make_async_copy(gate_in, gate, local.at[3]),
    ]
    for c in loads:
        c.start()

    barrier = pltpu.get_barrier_semaphore()

    @pl.loop(1, SEQ)
    def _(i):
        pl.semaphore_signal(
            barrier, inc=1, device_id={"seq": lax.rem(me + i, SEQ)}, device_id_type=MESH
        )

    for t in (zp, yp, ym):
        pl.semaphore_signal(barrier, inc=1, device_id={"tensor": t}, device_id_type=MESH)

    @pl.loop(0, 8)
    def _(r):
        i = iota((64, 512), 0) + r * 64
        n = iota((64, 512), 1)
        same = ((i >> 7) == ((n >> 5) & 3)) & (((i >> 5) & 3) == (n >> 7)) & ((i & 31) == (n & 31))
        perm[pl.ds(pl.multiple_of(r * 64, 64), 64), :] = jnp.where(same, 1.0, 0.0).astype(BF16)

    def remote(src, dst, ss, rs, dev, axis="seq"):
        return pltpu.make_async_remote_copy(
            src_ref=src, dst_ref=dst, send_sem=ss, recv_sem=rs,
            device_id={axis: dev}, device_id_type=MESH,
        )

    def lanes(i):
        return pl.ds(pl.multiple_of(i * QUARTER, QUARTER), QUARTER)

    def deliver(dest, part, staged, landed, ss, rs):
        staged[dest] = part

        @pl.when(dest != me)
        def _():
            remote(staged.at[dest], landed.at[me], ss.at[dest], rs.at[me], dest).start()

        @pl.when(dest == me)
        def _():
            landed[me] = part

    def collect(landed, staged, ss, rs):
        @pl.loop(1, SEQ)
        def _(i):
            src = lax.rem(me + i, SEQ)
            remote(staged.at[src], landed.at[src], ss.at[src], rs.at[src], src).wait_recv()

    def settle(landed, staged, ss, rs):
        @pl.loop(1, SEQ)
        def _(i):
            src = lax.rem(me + i, SEQ)
            remote(staged.at[src], landed.at[src], ss.at[src], rs.at[src], src).wait_send()

    def node(dx, dz, other=False):
        c = 1 - core if other else core
        return lax.rem(x + dx, 4) * 8 + lax.rem(zh + dz, 4) * 2 + c

    sent = []

    def push(block, dev):
        index = len(sent)
        c = remote(wv.at[block], wv.at[block], wsend.at[index], wrecv.at[block], dev)
        sent.append(c)
        return c

    def pushed(block):
        remote(wv.at[block], wv.at[block], wsend.at[0], wrecv.at[block], node(0, 0, True)).wait_recv()

    def spread(dz):
        block = node(0, dz)
        for dev in (node(1, 0), node(3, 0), node(0, 0, True)):
            push(block, dev).start()

    def onward(dz):
        for dx in (3, 1):
            pushed(node(dx, dz))
            push(node(dx, dz), node(0, 0, True)).start()
        block = jnp.where(first_core, node(3, dz), node(1, dz))
        push(block, jnp.where(first_core, node(1, 0), node(3, 0))).start()

    loads[0].wait()
    pl.semaphore_wait(barrier, SEQ - 1 + 3)

    @pl.loop(0, OUTER)
    def _(i):
        tile = lax.rem(me // INNER + i, OUTER)
        parts = [kv[QUARTER * k : QUARTER * (k + 1), lanes(tile)] for k in range(INNER)]
        for q, part in enumerate(swap(parts, perm)):
            deliver(tile * INNER + q, part, xs, xr, xsend, xrecv)

    loads[2].wait()

    @pl.loop(0, OUTER)
    def _(i):
        tile = lax.rem(me // INNER + i, OUTER)
        parts = []
        for k in range(INNER):
            pair = [
                filt[pl.ds(m * 1024 + 256 * k + tile, UNIT, stride=8), :].astype(BF16)
                for m in range(2)
            ]
            parts.append(jnp.concatenate(pair, axis=0))
        for q, part in enumerate(swap(parts, perm)):
            deliver(tile * INNER + q, part, fs, fr, fsend, frecv)

    loads[1].wait()
    spread(0)

    @pl.loop(0, KEPT // STEP)
    def _(r):
        rows = pl.ds(pl.multiple_of(r * STEP, STEP), STEP)
        more = pl.ds(pl.multiple_of(r * STEP + KEPT, STEP), STEP)
        phase = kcol[rows, 0:1] * iota((STEP, TOK), 1)
        ch, cl = halves(cosine_of(phase))
        sn = cosine_of(phase - 128)
        sh, sl = halves(sn)
        nh, nl = halves(-sn)
        mh[rows, 0:TOK] = ch
        ml[rows, 0:TOK] = cl
        mh[rows, TOK:] = sh
        ml[rows, TOK:] = sl
        mh[more, 0:TOK] = nh
        ml[more, 0:TOK] = nl
        mh[more, TOK:] = ch
        ml[more, TOK:] = cl

    @pl.loop(0, TOK // 64)
    def _(r):
        rows = pl.ds(pl.multiple_of(r * 64, 64), 64)
        more = pl.ds(pl.multiple_of(r * 64 + TOK, 64), 64)
        phase = krow[0:1, :] * (iota((64, KEPT), 0) + r * 64)
        ch, cl = halves(cosine_of(phase))
        sn = cosine_of(phase - 128)
        sh, sl = halves(sn)
        nh, nl = halves(-sn)
        th[rows, 0:KEPT] = ch
        tl[rows, 0:KEPT] = cl
        th[rows, KEPT:] = nh
        tl[rows, KEPT:] = nl
        th[more, 0:KEPT] = sh
        tl[more, 0:KEPT] = sl
        th[more, KEPT:] = ch
        tl[more, KEPT:] = cl

    @pl.loop(0, OUTER)
    def _(a):
        i, n = iota((128, 256), 0), iota((128, 256), 1)
        phase = ((i >> 5) * 8 + a) * ((n >> 5) & 3) + 8 * (n >> 7)
        hi, lo = halves(jnp.where((i & 31) == (n & 31), cosine_of(phase * 16), 0.0))
        dm[a, 0:128, :] = hi
        dm[a, 128:256, :] = lo
        n, i = iota((256, 128), 0), iota((256, 128), 1)
        phase = ((i >> 5) * 8 + a) * ((n >> 5) & 3) + 8 * (n >> 7)
        hi, lo = halves(jnp.where((i & 31) == (n & 31), cosine_of(phase * 16), 0.0))
        eh[a] = hi
        el[a] = lo

    @pl.loop(0, ROWS)
    def _(r):
        rows = pl.ds(pl.multiple_of(r * STEP, STEP), STEP)
        j = iota((STEP, 128), 0) + r * STEP
        alpha = (j * (iota((STEP, 128), 1) >> 5)).astype(F32) * (2 * math.pi / LENGTH)
        beta = (j * INNER).astype(F32) * (2 * math.pi / LENGTH)
        tw[0, rows, :] = sine(math.pi / 2 - alpha)
        tw[1, rows, :] = sine(alpha)
        tw[2, rows, :] = sine(math.pi / 2 - beta)
        tw[3, rows, :] = sine(beta)

    collect(xr, xs, xsend, xrecv)
    for dz in (1, 3):
        push(me, node(0, dz)).start()

    @pl.loop(0, OUTER)
    def _(a):
        for k, part in enumerate(swap([xr[OUTER * l + a] for l in range(INNER)], perm)):
            rq[QUARTER * k : QUARTER * (k + 1), 0:128] = part
            rq[QUARTER * k : QUARTER * (k + 1), 128:256] = part
        g[a] = dot(rq[...], dm[a])

    def twists(rows):
        tc, ts = tw[0, rows, :], tw[1, rows, :]
        uc, us = tw[2, rows, :], tw[3, rows, :]
        found = []
        for p in range(OUTER):
            found.append((tc, ts))
            if p + 1 < OUTER:
                tc, ts = tc * uc - ts * us, ts * uc + tc * us
        return found

    @pl.loop(0, ROWS)
    def _(r):
        rows = pl.ds(pl.multiple_of(r * STEP, STEP), STEP)
        more = pl.ds(pl.multiple_of(r * STEP + TOK, STEP), STEP)
        first = transform([(g[a, rows, 0:128], g[a, rows, 128:256]) for a in range(OUTER)], -1)
        for p, ((re, im), (tc, ts)) in enumerate(zip(first, twists(rows))):
            cols = slice(128 * (p % 2), 128 * (p % 2) + 128)
            fst[p // 2, rows, cols] = (re * tc + im * ts).astype(BF16)
            fst[p // 2, more, cols] = (im * tc - re * ts).astype(BF16)

    collect(fr, fs, fsend, frecv)

    @pl.loop(0, OUTER // 2)
    def _(w):
        for half in range(2):
            p = 2 * w + half
            cols = slice(128 * half, 128 * half + 128)
            for k, part in enumerate(swap([fr[INNER * p + l] for l in range(INNER)], perm)):
                fm[0, UNIT * k : UNIT * (k + 1), cols] = part[0:UNIT]
                fm[1, UNIT * k : UNIT * (k + 1), cols] = part[UNIT:]
        spectrum = dot(mh[...], fst[w]) + dot(ml[...], fst[w])
        sr, si = spectrum[0:KEPT], spectrum[KEPT:]
        f_re, f_im = fm[0].astype(F32), fm[1].astype(F32)
        product = jnp.concatenate([f_re * sr - f_im * si, f_re * si + f_im * sr], axis=0)
        hi, lo = halves(product)
        for part in range(2):
            rows = slice(TOK * part, TOK * (part + 1))
            g[2 * w + part] = dot(th[rows], hi) + dot(tl[rows], hi) + dot(th[rows], lo)

    @pl.loop(0, ROWS)
    def _(r):
        rows = pl.ds(pl.multiple_of(r * STEP, STEP), STEP)
        turned = []
        for p, (tc, ts) in enumerate(twists(rows)):
            cols = slice(128 * (p % 2), 128 * (p % 2) + 128)
            re, im = g[p // 2 * 2, rows, cols], g[p // 2 * 2 + 1, rows, cols]
            turned.append(
                (
                    (re * tc - im * ts).astype(BF16).astype(F32),
                    (re * ts + im * tc).astype(BF16).astype(F32),
                )
            )
        for a, (re, im) in enumerate(transform(turned, 1)):
            hi, lo = halves(re)
            vh[a, rows, 0:128] = hi
            vl[a, rows, 0:128] = lo
            hi, lo = halves(im)
            vh[a, rows, 128:256] = hi
            vl[a, rows, 128:256] = lo

    @pl.loop(0, OUTER)
    def _(i):
        a = lax.rem(lax.rem(me, OUTER) + i, OUTER)
        c = dot(vh[a], eh[a]) + dot(vl[a], eh[a]) + dot(vh[a], el[a])
        c = (c * (1.0 / LENGTH)).astype(BF16)
        for l, part in enumerate(swap([c[QUARTER * k : QUARTER * (k + 1)] for k in range(INNER)], perm)):
            deliver(OUTER * l + a, part, cs, cr, csend, crecv)

    for dz in (3, 1):
        pushed(node(0, dz))
    push(
        jnp.where(first_core, node(0, 3), node(0, 1)),
        jnp.where(first_core, node(0, 1), node(0, 3)),
    ).start()
    spread(1)
    spread(3)
    onward(0)
    loads[3].wait()

    collect(cr, cs, csend, crecv)
    hid = gath.at[ten]

    @pl.loop(0, OUTER)
    def _(tile):
        for k, part in enumerate(swap([cr[INNER * tile + q] for q in range(INNER)], perm)):
            rows = slice(QUARTER * k, QUARTER * (k + 1))
            direct = skip[0:1, lanes(tile)] * kv[rows, lanes(tile)].astype(F32)
            hid[rows, lanes(tile)] = (
                gate[rows, lanes(tile)].astype(F32) * (part.astype(F32) + direct)
            ).astype(BF16)

    every, upper, lower = slice(0, TOK), slice(0, SPLIT), slice(SPLIT, TOK)
    gathers = []

    def gather(block, rows, to, side=0):
        c = remote(
            gath.at[block, rows], gath.at[block, rows],
            gsend.at[len(gathers)], grecv.at[side, block], to, "tensor",
        )
        gathers.append(c)
        c.start()

    def arrived(block, rows, side=0):
        remote(
            gath.at[block, rows], gath.at[block, rows],
            gsend.at[0], grecv.at[side, block], zp, "tensor",
        ).wait_recv()

    gather(ten, every, yp)
    gather(ten, every, ym)
    gather(ten, every, zp)
    pushed(node(0, 2))
    spread(2)
    arrived(zp, every)
    gather(zp, upper, yp)
    gather(zp, upper, ym)
    ahead = jnp.where(first_core, yp, ym)
    arrived(ym, every)
    arrived(yp, every)
    gather(jnp.where(first_core, ym, yp), every, ahead)
    gather(ym, lower, zp, 1)
    gather(yp, lower, zp, 1)
    onward(1)
    onward(3)
    onward(2)
    arrived(far + down, upper)
    arrived(far + up, upper)
    gather(jnp.where(first_core, far + down, far + up), upper, ahead)
    arrived(near + across, every)
    gather(near + across, lower, zp, 1)
    for dz in range(4):
        pushed(node(2, dz))
        push(node(2, dz), node(0, 0, True)).start()
    for dx in range(4):
        for dz in range(4):
            pushed(node(dx, dz, True))

    def project(block, start=False):
        @pl.loop(0, 4)
        def _(n):
            cols = pl.ds(pl.multiple_of(n * 256, 256), 256)
            w = wv[pl.ds(INNER * block, INNER), :, cols].reshape(WIDTH, 256)
            part = dot(gath[block], w)
            acc[:, cols] = part if start else acc[:, cols] + part

    project(ten, True)
    project(zp)
    project(ym)
    project(yp)
    project(near + across)
    for block in (far + down, far + up):
        arrived(block, lower, 1)
        project(block)
    arrived(far + across, upper)
    arrived(far + across, lower, 1)
    project(far + across)
    out[...] = acc[...].astype(BF16)
    for c in gathers:
        c.wait_send()
    for c in sent:
        c.wait_send()
    settle(xr, xs, xsend, xrecv)
    settle(fr, fs, fsend, frecv)
    settle(cr, cs, csend, crecv)


def body(keyval, gating, skip_gain, filter_values, blocks, out_weight):
    me = lax.axis_index("seq")
    groups = blocks.shape[0]
    match = me * groups // SEQ == jnp.arange(groups, dtype=jnp.int32)
    kept = jnp.sum(jnp.where(match[:, None], blocks, 0), axis=0)
    kept = (kept[:, None] * 2 + jnp.arange(2, dtype=jnp.int32)[None, :]).reshape(KEPT)
    kcol = jnp.broadcast_to(kept[:, None], (KEPT, 128))
    krow = jnp.broadcast_to(kept[None, :], (8, KEPT))
    vmem = pl.BlockSpec(memory_space=pltpu.VMEM)
    away = pl.BlockSpec(memory_space=pl.ANY)
    dma = pltpu.SemaphoreType.DMA

    def buf(*shape, dtype=BF16):
        return pltpu.VMEM(shape, dtype)

    return pl.pallas_call(
        kernel,
        out_shape=jax.ShapeDtypeStruct((TOK, WIDTH), BF16),
        in_specs=[away, away, vmem, away, vmem, vmem, away],
        out_specs=vmem,
        scratch_shapes=[
            buf(TOK, WIDTH), buf(TOK, WIDTH), buf(2048, 128, dtype=F32),
            buf(SEQ, 128, 128), buf(SEQ, 128, 128),
            buf(SEQ, 64, 128), buf(SEQ, 64, 128),
            buf(256, 1024), buf(256, 1024), buf(1024, 256), buf(1024, 256),
            buf(8, 256, 256), buf(8, 256, 128), buf(8, 256, 128), buf(512, 512),
            buf(4, 512, 128, dtype=F32), buf(512, 256), buf(8, 512, 256, dtype=F32),
            buf(4, 1024, 256), buf(2, 128, 256),
            buf(8, 512, 256), buf(8, 512, 256),
            buf(SEQ, 128, 128), buf(SEQ, 128, 128), buf(8, TOK, WIDTH),
            buf(SEQ, 256, WIDTH), buf(TOK, WIDTH, dtype=F32),
            dma((SEQ,)), dma((SEQ,)), dma((SEQ,)), dma((SEQ,)), dma((SEQ,)), dma((SEQ,)),
            dma((10,)), dma((2, 8)), dma((31,)), dma((SEQ,)), dma((4,)),
        ],
        compiler_params=pltpu.CompilerParams(
            collective_id=0, has_side_effects=True, vmem_limit_bytes=60 * 2**20
        ),
    )(
        keyval, gating, skip_gain.reshape(1, WIDTH), filter_values.reshape(2048, 128),
        kcol, krow, out_weight,
    )


def solution(mesh):
    placed = (
        P("seq", "tensor"),
        P("seq", "tensor"),
        P("tensor"),
        P(None, None, None, "seq", "tensor"),
        P("tensor", None),
        P("seq", "tensor"),
    )
    return jax.shard_map(
        body, mesh=mesh, in_specs=placed, out_specs=P("seq", "tensor"), check_vma=False
    )
```

```python
import math

import jax
import jax.numpy as jnp
from jax import lax
from jax.experimental import pallas as pl
from jax.experimental.pallas import tpu as pltpu
from jax.sharding import PartitionSpec as P

BLOCK = 64
SEQ = 32
OUTER = 8
INNER = 4
TOK = 512
QUARTER = 128
WIDTH = 1024
UNIT = 32
KEPT = 128
STEP = 16
ROWS = TOK // STEP
HALF = TOK // 2
LENGTH = SEQ * TOK
F32 = jnp.float32
BF16 = jnp.bfloat16
MESH = pl.DeviceIdType.MESH


def iota(shape, axis):
    return lax.broadcasted_iota(jnp.int32, shape, axis)


def sine(x):
    s = x * x
    t = -1.0 / 39916800.0
    for c in (1.0 / 362880.0, -1.0 / 5040.0, 1.0 / 120.0, -1.0 / 6.0, 1.0):
        t = t * s + c
    return x * t


def cosine_of(phase):
    d = jnp.abs((phase & 511) - 256) - 128
    return sine(d.astype(F32) * (math.pi / 256.0))


def halves(v):
    hi = v.astype(BF16)
    return hi, (v - hi.astype(F32)).astype(BF16)


def dot(a, b):
    return jnp.dot(a, b, preferred_element_type=F32)


def turn(v, num, den, sign):
    re, im = v
    num = num % den
    if num == 0:
        return v
    if 4 * num == den:
        return (-im, re) if sign > 0 else (im, -re)
    c = math.cos(2 * math.pi * num / den)
    s = sign * math.sin(2 * math.pi * num / den)
    if 8 * num == den:
        h = c
        return (h * (re - im), h * (re + im)) if sign > 0 else (h * (re + im), h * (im - re))
    if 8 * num == 3 * den:
        h = -c
        return (-h * (re + im), h * (re - im)) if sign > 0 else (h * (im - re), -h * (re + im))
    return (re * c - im * s, re * s + im * c)


def transform(values, sign):
    n = len(values)
    if n == 1:
        return values
    even = transform(values[0::2], sign)
    odd = transform(values[1::2], sign)
    odd = [turn(o, k, n, sign) for k, o in enumerate(odd)]
    low = [(e[0] + o[0], e[1] + o[1]) for e, o in zip(even, odd)]
    high = [(e[0] - o[0], e[1] - o[1]) for e, o in zip(even, odd)]
    return low + high


def swap(parts, perm):
    u = dot(jnp.concatenate(parts, axis=1), perm[...]).astype(BF16)
    return [u[:, QUARTER * i : QUARTER * (i + 1)] for i in range(INNER)]


def kernel(
    kv_in, gate_in, skip, filt_in, blocks, weight_in, out,
    kcol, krow, kv, gate, filt, xs, xr, fs, fr, mh, ml, th, tl, dm, eh, el, perm, tw, rq, g, fst, fm, vh, vl,
    cs, cr, gath, wv, acc,
    xsend, xrecv, fsend, frecv, csend, crecv, gsend, grecv, wsend, wrecv, local,
):
    me = lax.axis_index("seq")
    ten = lax.axis_index("tensor")
    zl, y = ten // 4, lax.rem(ten, 4)
    far, near = (1 - zl) * 4, zl * 4
    zp = far + y
    up, down, across = lax.rem(y + 1, 4), lax.rem(y + 3, 4), lax.rem(y + 2, 4)
    yp, ym = near + up, near + down
    core = lax.rem(me, 2)
    zh = lax.rem(me // 2, 4)
    x = me // 8
    first_core = core == 0

    loads = [
        pltpu.make_async_copy(kv_in, kv, local.at[0]),
        pltpu.make_async_copy(weight_in, wv.at[me], local.at[1]),
        pltpu.make_async_copy(filt_in, filt, local.at[2]),
        pltpu.make_async_copy(gate_in, gate, local.at[3]),
    ]
    for c in loads:
        c.start()

    barrier = pltpu.get_barrier_semaphore()

    @pl.loop(1, SEQ)
    def _(i):
        pl.semaphore_signal(
            barrier, inc=1, device_id={"seq": lax.rem(me + i, SEQ)}, device_id_type=MESH
        )

    for t in (zp, yp, ym):
        pl.semaphore_signal(barrier, inc=1, device_id={"tensor": t}, device_id_type=MESH)

    @pl.loop(0, 8)
    def _(r):
        i = iota((64, 512), 0) + r * 64
        n = iota((64, 512), 1)
        same = ((i >> 7) == ((n >> 5) & 3)) & (((i >> 5) & 3) == (n >> 7)) & ((i & 31) == (n & 31))
        perm[pl.ds(pl.multiple_of(r * 64, 64), 64), :] = jnp.where(same, 1.0, 0.0).astype(BF16)

    def remote(src, dst, ss, rs, dev, axis="seq"):
        return pltpu.make_async_remote_copy(
            src_ref=src, dst_ref=dst, send_sem=ss, recv_sem=rs,
            device_id={axis: dev}, device_id_type=MESH,
        )

    def lanes(i):
        return pl.ds(pl.multiple_of(i * QUARTER, QUARTER), QUARTER)

    def deliver(dest, part, staged, landed, ss, rs):
        staged[dest] = part

        @pl.when(dest != me)
        def _():
            remote(staged.at[dest], landed.at[me], ss.at[dest], rs.at[me], dest).start()

        @pl.when(dest == me)
        def _():
            landed[me] = part

    def collect(landed, staged, ss, rs):
        @pl.loop(1, SEQ)
        def _(i):
            src = lax.rem(me + i, SEQ)
            remote(staged.at[src], landed.at[src], ss.at[src], rs.at[src], src).wait_recv()

    def settle(landed, staged, ss, rs):
        @pl.loop(1, SEQ)
        def _(i):
            src = lax.rem(me + i, SEQ)
            remote(staged.at[src], landed.at[src], ss.at[src], rs.at[src], src).wait_send()

    def node(dx, dz, other=False):
        c = 1 - core if other else core
        return lax.rem(x + dx, 4) * 8 + lax.rem(zh + dz, 4) * 2 + c

    sent = []

    def push(block, dev):
        index = len(sent)
        c = remote(wv.at[block], wv.at[block], wsend.at[index], wrecv.at[block], dev)
        sent.append(c)
        return c

    def pushed(block):
        remote(wv.at[block], wv.at[block], wsend.at[0], wrecv.at[block], node(0, 0, True)).wait_recv()

    def spread(dz):
        block = node(0, dz)
        for dev in (node(1, 0), node(3, 0), node(0, 0, True)):
            push(block, dev).start()

    def onward(dz):
        for dx in (3, 1):
            pushed(node(dx, dz))
            push(node(dx, dz), node(0, 0, True)).start()
        block = jnp.where(first_core, node(3, dz), node(1, dz))
        push(block, jnp.where(first_core, node(1, 0), node(3, 0))).start()

    loads[0].wait()
    pl.semaphore_wait(barrier, SEQ - 1 + 3)

    @pl.loop(0, OUTER)
    def _(i):
        tile = lax.rem(me // INNER + i, OUTER)
        parts = [kv[QUARTER * k : QUARTER * (k + 1), lanes(tile)] for k in range(INNER)]
        for q, part in enumerate(swap(parts, perm)):
            deliver(tile * INNER + q, part, xs, xr, xsend, xrecv)

    loads[2].wait()

    @pl.loop(0, OUTER)
    def _(i):
        tile = lax.rem(me // INNER + i, OUTER)
        parts = []
        for k in range(INNER):
            pair = [
                filt[pl.ds(m * 1024 + 256 * k + tile, UNIT, stride=8), :].astype(BF16)
                for m in range(2)
            ]
            parts.append(jnp.concatenate(pair, axis=0))
        for q, part in enumerate(swap(parts, perm)):
            deliver(tile * INNER + q, part, fs, fr, fsend, frecv)

    loads[1].wait()
    spread(0)

    group = iota((OUTER, 64), 0) == me // INNER
    listed = jnp.sum(jnp.where(group, blocks[...].astype(F32), 0.0), axis=0, keepdims=True)
    own = iota((KEPT, 64), 1) == (iota((KEPT, 64), 0) >> 1)
    column = jnp.sum(jnp.where(own, listed, 0.0), axis=1, keepdims=True)
    column = column.astype(jnp.int32) * 2 + (iota((KEPT, 1), 0) & 1)
    kcol[...] = jnp.broadcast_to(column, (KEPT, 128))
    own = iota((64, 64), 1) == iota((64, 64), 0)
    upright = jnp.sum(jnp.where(own, listed, 0.0), axis=1, keepdims=True)
    own = iota((64, KEPT), 0) == (iota((64, KEPT), 1) >> 1)
    row = jnp.sum(jnp.where(own, upright, 0.0), axis=0, keepdims=True)
    row = row.astype(jnp.int32) * 2 + (iota((1, KEPT), 1) & 1)
    krow[...] = jnp.broadcast_to(row, (8, KEPT))

    @pl.loop(0, KEPT // STEP)
    def _(r):
        rows = pl.ds(pl.multiple_of(r * STEP, STEP), STEP)
        more = pl.ds(pl.multiple_of(r * STEP + KEPT, STEP), STEP)
        phase = kcol[rows, 0:1] * iota((STEP, TOK), 1)
        ch, cl = halves(cosine_of(phase))
        sn = cosine_of(phase - 128)
        sh, sl = halves(sn)
        nh, nl = halves(-sn)
        mh[rows, 0:TOK] = ch
        ml[rows, 0:TOK] = cl
        mh[rows, TOK:] = sh
        ml[rows, TOK:] = sl
        mh[more, 0:TOK] = nh
        ml[more, 0:TOK] = nl
        mh[more, TOK:] = ch
        ml[more, TOK:] = cl

    @pl.loop(0, TOK // 64)
    def _(r):
        rows = pl.ds(pl.multiple_of(r * 64, 64), 64)
        more = pl.ds(pl.multiple_of(r * 64 + TOK, 64), 64)
        phase = krow[0:1, :] * (iota((64, KEPT), 0) + r * 64)
        ch, cl = halves(cosine_of(phase))
        sn = cosine_of(phase - 128)
        sh, sl = halves(sn)
        nh, nl = halves(-sn)
        th[rows, 0:KEPT] = ch
        tl[rows, 0:KEPT] = cl
        th[rows, KEPT:] = nh
        tl[rows, KEPT:] = nl
        th[more, 0:KEPT] = sh
        tl[more, 0:KEPT] = sl
        th[more, KEPT:] = ch
        tl[more, KEPT:] = cl

    @pl.loop(0, OUTER)
    def _(a):
        i, n = iota((128, 256), 0), iota((128, 256), 1)
        phase = ((i >> 5) * 8 + a) * ((n >> 5) & 3) + 8 * (n >> 7)
        hi, lo = halves(jnp.where((i & 31) == (n & 31), cosine_of(phase * 16), 0.0))
        dm[a, 0:128, :] = hi
        dm[a, 128:256, :] = lo
        n, i = iota((256, 128), 0), iota((256, 128), 1)
        phase = ((i >> 5) * 8 + a) * ((n >> 5) & 3) + 8 * (n >> 7)
        hi, lo = halves(jnp.where((i & 31) == (n & 31), cosine_of(phase * 16), 0.0))
        eh[a] = hi
        el[a] = lo

    @pl.loop(0, ROWS)
    def _(r):
        rows = pl.ds(pl.multiple_of(r * STEP, STEP), STEP)
        j = iota((STEP, 128), 0) + r * STEP
        alpha = (j * (iota((STEP, 128), 1) >> 5)).astype(F32) * (2 * math.pi / LENGTH)
        beta = (j * INNER).astype(F32) * (2 * math.pi / LENGTH)
        tw[0, rows, :] = sine(math.pi / 2 - alpha)
        tw[1, rows, :] = sine(alpha)
        tw[2, rows, :] = sine(math.pi / 2 - beta)
        tw[3, rows, :] = sine(beta)

    collect(xr, xs, xsend, xrecv)
    for dz in (1, 3):
        push(me, node(0, dz)).start()

    @pl.loop(0, OUTER)
    def _(a):
        for k, part in enumerate(swap([xr[OUTER * l + a] for l in range(INNER)], perm)):
            rq[QUARTER * k : QUARTER * (k + 1), 0:128] = part
            rq[QUARTER * k : QUARTER * (k + 1), 128:256] = part
        g[a] = dot(rq[...], dm[a])

    def twists(rows):
        tc, ts = tw[0, rows, :], tw[1, rows, :]
        uc, us = tw[2, rows, :], tw[3, rows, :]
        found = []
        for p in range(OUTER):
            found.append((tc, ts))
            if p + 1 < OUTER:
                tc, ts = tc * uc - ts * us, ts * uc + tc * us
        return found

    @pl.loop(0, ROWS)
    def _(r):
        rows = pl.ds(pl.multiple_of(r * STEP, STEP), STEP)
        more = pl.ds(pl.multiple_of(r * STEP + TOK, STEP), STEP)
        first = transform([(g[a, rows, 0:128], g[a, rows, 128:256]) for a in range(OUTER)], -1)
        for p, ((re, im), (tc, ts)) in enumerate(zip(first, twists(rows))):
            cols = slice(128 * (p % 2), 128 * (p % 2) + 128)
            fst[p // 2, rows, cols] = (re * tc + im * ts).astype(BF16)
            fst[p // 2, more, cols] = (im * tc - re * ts).astype(BF16)

    collect(fr, fs, fsend, frecv)

    @pl.loop(0, OUTER // 2)
    def _(w):
        for half in range(2):
            p = 2 * w + half
            cols = slice(128 * half, 128 * half + 128)
            for k, part in enumerate(swap([fr[INNER * p + l] for l in range(INNER)], perm)):
                fm[0, UNIT * k : UNIT * (k + 1), cols] = part[0:UNIT]
                fm[1, UNIT * k : UNIT * (k + 1), cols] = part[UNIT:]
        spectrum = dot(mh[...], fst[w]) + dot(ml[...], fst[w])
        sr, si = spectrum[0:KEPT], spectrum[KEPT:]
        f_re, f_im = fm[0].astype(F32), fm[1].astype(F32)
        product = jnp.concatenate([f_re * sr - f_im * si, f_re * si + f_im * sr], axis=0)
        hi, lo = halves(product)
        for part in range(2):
            rows = slice(TOK * part, TOK * (part + 1))
            g[2 * w + part] = dot(th[rows], hi) + dot(tl[rows], hi) + dot(th[rows], lo)

    for half in range(2):

        @pl.loop(half * (ROWS // 2), (half + 1) * (ROWS // 2))
        def _(r):
            rows = pl.ds(pl.multiple_of(r * STEP, STEP), STEP)
            turned = []
            for p, (tc, ts) in enumerate(twists(rows)):
                cols = slice(128 * (p % 2), 128 * (p % 2) + 128)
                re, im = g[p // 2 * 2, rows, cols], g[p // 2 * 2 + 1, rows, cols]
                turned.append(
                    (
                        (re * tc - im * ts).astype(BF16).astype(F32),
                        (re * ts + im * tc).astype(BF16).astype(F32),
                    )
                )
            for a, (re, im) in enumerate(transform(turned, 1)):
                hi, lo = halves(re)
                vh[a, rows, 0:128] = hi
                vl[a, rows, 0:128] = lo
                hi, lo = halves(im)
                vh[a, rows, 128:256] = hi
                vl[a, rows, 128:256] = lo

        @pl.loop(0, OUTER)
        def _(i):
            a = lax.rem(lax.rem(me, OUTER) + i, OUTER)
            rows = slice(HALF * half, HALF * (half + 1))
            v, rest = vh[a, rows], vl[a, rows]
            c = dot(v, eh[a]) + dot(rest, eh[a]) + dot(v, el[a])
            c = (c * (1.0 / LENGTH)).astype(BF16)
            parts = [c[64 * k : 64 * (k + 1)] for k in range(INNER)]
            for l, part in enumerate(swap(parts, perm)):
                deliver(
                    OUTER * l + a, part, cs.at[half], cr.at[half], csend.at[half], crecv.at[half]
                )

    for dz in (3, 1):
        pushed(node(0, dz))
    push(
        jnp.where(first_core, node(0, 3), node(0, 1)),
        jnp.where(first_core, node(0, 1), node(0, 3)),
    ).start()
    spread(1)
    spread(3)
    onward(0)
    loads[3].wait()

    hid = gath.at[ten]
    gathers = []
    whole = [slice(HALF * half, HALF * (half + 1)) for half in range(2)]
    ahead = jnp.where(first_core, yp, ym)

    def gather(half, block, to):
        c = remote(
            gath.at[block, whole[half]], gath.at[block, whole[half]],
            gsend.at[len(gathers)], grecv.at[half, block], to, "tensor",
        )
        gathers.append(c)
        c.start()

    def arrived(half, block):
        remote(
            gath.at[block, whole[half]], gath.at[block, whole[half]],
            gsend.at[0], grecv.at[half, block], zp, "tensor",
        ).wait_recv()

    def settled(half):
        collect(cr.at[half], cs.at[half], csend.at[half], crecv.at[half])

        @pl.loop(0, OUTER)
        def _(tile):
            parts = [cr[half, INNER * tile + q] for q in range(INNER)]
            for k, part in enumerate(swap(parts, perm)):
                rows = slice(HALF * half + 64 * k, HALF * half + 64 * (k + 1))
                direct = skip[0:1, lanes(tile)] * kv[rows, lanes(tile)].astype(F32)
                hid[rows, lanes(tile)] = (
                    gate[rows, lanes(tile)].astype(F32) * (part.astype(F32) + direct)
                ).astype(BF16)

        for to in (yp, ym, zp):
            gather(half, ten, to)

    def cross(half):
        arrived(half, zp)
        gather(half, zp, yp)
        gather(half, zp, ym)

    def ring(half):
        arrived(half, ym)
        arrived(half, yp)
        gather(half, jnp.where(first_core, ym, yp), ahead)

    def distant(half):
        arrived(half, far + down)
        arrived(half, far + up)
        gather(half, jnp.where(first_core, far + down, far + up), ahead)

    settled(0)
    settled(1)
    ring(0)
    cross(0)
    pushed(node(0, 2))
    spread(2)
    ring(1)
    cross(1)
    onward(1)
    onward(3)
    distant(0)
    onward(2)
    for dz in range(4):
        pushed(node(2, dz))
        push(node(2, dz), node(0, 0, True)).start()
    distant(1)
    for dx in range(4):
        for dz in range(4):
            pushed(node(dx, dz, True))

    def project(block, start=False):
        @pl.loop(0, 4)
        def _(n):
            cols = pl.ds(pl.multiple_of(n * 256, 256), 256)
            w = wv[pl.ds(INNER * block, INNER), :, cols].reshape(WIDTH, 256)
            part = dot(gath[block], w)
            acc[:, cols] = part if start else acc[:, cols] + part

    project(ten, True)
    project(zp)
    project(ym)
    project(yp)
    project(far + down)
    project(far + up)
    for block in (near + across, far + across):
        for half in range(2):
            arrived(half, block)
        project(block)
    out[...] = acc[...].astype(BF16)
    for c in gathers:
        c.wait_send()
    for c in sent:
        c.wait_send()
    settle(xr, xs, xsend, xrecv)
    settle(fr, fs, fsend, frecv)
    for half in range(2):
        settle(cr.at[half], cs.at[half], csend.at[half], crecv.at[half])


def body(keyval, gating, skip_gain, filter_values, blocks, out_weight):
    vmem = pl.BlockSpec(memory_space=pltpu.VMEM)
    away = pl.BlockSpec(memory_space=pl.ANY)
    dma = pltpu.SemaphoreType.DMA

    def buf(*shape, dtype=BF16):
        return pltpu.VMEM(shape, dtype)

    return pl.pallas_call(
        kernel,
        out_shape=jax.ShapeDtypeStruct((TOK, WIDTH), BF16),
        in_specs=[away, away, vmem, away, vmem, away],
        out_specs=vmem,
        scratch_shapes=[
            buf(KEPT, 128, dtype=jnp.int32), buf(8, KEPT, dtype=jnp.int32),
            buf(TOK, WIDTH), buf(TOK, WIDTH), buf(2048, 128, dtype=F32),
            buf(SEQ, 128, 128), buf(SEQ, 128, 128),
            buf(SEQ, 64, 128), buf(SEQ, 64, 128),
            buf(256, 1024), buf(256, 1024), buf(1024, 256), buf(1024, 256),
            buf(8, 256, 256), buf(8, 256, 128), buf(8, 256, 128), buf(512, 512),
            buf(4, 512, 128, dtype=F32), buf(512, 256), buf(8, 512, 256, dtype=F32),
            buf(4, 1024, 256), buf(2, 128, 256),
            buf(8, 512, 256), buf(8, 512, 256),
            buf(2, SEQ, 64, 128), buf(2, SEQ, 64, 128), buf(8, TOK, WIDTH),
            buf(SEQ, 256, WIDTH), buf(TOK, WIDTH, dtype=F32),
            dma((SEQ,)), dma((SEQ,)), dma((SEQ,)), dma((SEQ,)), dma((2, SEQ)), dma((2, SEQ)),
            dma((14,)), dma((2, 8)), dma((31,)), dma((SEQ,)), dma((4,)),
        ],
        compiler_params=pltpu.CompilerParams(
            collective_id=0, has_side_effects=True, vmem_limit_bytes=60 * 2**20
        ),
    )(
        keyval, gating, skip_gain.reshape(1, WIDTH), filter_values.reshape(2048, 128),
        blocks, out_weight,
    )


def solution(mesh):
    placed = (
        P("seq", "tensor"),
        P("seq", "tensor"),
        P("tensor"),
        P(None, None, None, "seq", "tensor"),
        P("tensor", None),
        P("seq", "tensor"),
    )
    return jax.shard_map(
        body, mesh=mesh, in_specs=placed, out_specs=P("seq", "tensor"), check_vma=False
    )
```

```python
import math

import jax
import jax.numpy as jnp
from jax import lax
from jax.experimental import pallas as pl
from jax.experimental.pallas import tpu as pltpu
from jax.sharding import PartitionSpec as P

BLOCK = 64
SEQ = 32
OUTER = 8
INNER = 4
TOK = 512
QUARTER = 128
WIDTH = 1024
UNIT = 32
KEPT = 128
STEP = 16
ROWS = TOK // STEP
HALF = TOK // 2
UPPER = 176
LENGTH = SEQ * TOK
F32 = jnp.float32
BF16 = jnp.bfloat16
MESH = pl.DeviceIdType.MESH


def iota(shape, axis):
    return lax.broadcasted_iota(jnp.int32, shape, axis)


def sine(x):
    s = x * x
    t = -1.0 / 39916800.0
    for c in (1.0 / 362880.0, -1.0 / 5040.0, 1.0 / 120.0, -1.0 / 6.0, 1.0):
        t = t * s + c
    return x * t


def cosine_of(phase):
    d = jnp.abs((phase & 511) - 256) - 128
    return sine(d.astype(F32) * (math.pi / 256.0))


def halves(v):
    hi = v.astype(BF16)
    return hi, (v - hi.astype(F32)).astype(BF16)


def dot(a, b):
    return jnp.dot(a, b, preferred_element_type=F32)


def turn(v, num, den, sign):
    re, im = v
    num = num % den
    if num == 0:
        return v
    if 4 * num == den:
        return (-im, re) if sign > 0 else (im, -re)
    c = math.cos(2 * math.pi * num / den)
    s = sign * math.sin(2 * math.pi * num / den)
    if 8 * num == den:
        h = c
        return (h * (re - im), h * (re + im)) if sign > 0 else (h * (re + im), h * (im - re))
    if 8 * num == 3 * den:
        h = -c
        return (-h * (re + im), h * (re - im)) if sign > 0 else (h * (im - re), -h * (re + im))
    return (re * c - im * s, re * s + im * c)


def transform(values, sign):
    n = len(values)
    if n == 1:
        return values
    even = transform(values[0::2], sign)
    odd = transform(values[1::2], sign)
    odd = [turn(o, k, n, sign) for k, o in enumerate(odd)]
    low = [(e[0] + o[0], e[1] + o[1]) for e, o in zip(even, odd)]
    high = [(e[0] - o[0], e[1] - o[1]) for e, o in zip(even, odd)]
    return low + high


def swap(parts, perm):
    u = dot(jnp.concatenate(parts, axis=1), perm[...]).astype(BF16)
    return [u[:, QUARTER * i : QUARTER * (i + 1)] for i in range(INNER)]


def kernel(
    kv_in, gate_in, skip, filt_in, blocks, weight_in, out,
    kcol, krow, kv, gate, filt, xs, xr, fs, fr, mh, ml, th, tl, dm, eh, el, perm, tw, rq, g, fst, fm, vh, vl,
    cs, cr, gath, wv, acc,
    xsend, xrecv, fsend, frecv, csend, crecv, gsend, grecv, wsend, wrecv, local,
):
    me = lax.axis_index("seq")
    ten = lax.axis_index("tensor")
    zl, y = ten // 4, lax.rem(ten, 4)
    far, near = (1 - zl) * 4, zl * 4
    zp = far + y
    up, down, across = lax.rem(y + 1, 4), lax.rem(y + 3, 4), lax.rem(y + 2, 4)
    yp, ym = near + up, near + down
    core = lax.rem(me, 2)
    zh = lax.rem(me // 2, 4)
    x = me // 8
    first_core = core == 0

    loads = [
        pltpu.make_async_copy(kv_in, kv, local.at[0]),
        pltpu.make_async_copy(weight_in, wv.at[me], local.at[1]),
        pltpu.make_async_copy(filt_in, filt, local.at[2]),
        pltpu.make_async_copy(gate_in, gate, local.at[3]),
    ]
    for c in loads:
        c.start()

    barrier = pltpu.get_barrier_semaphore()

    @pl.loop(1, SEQ)
    def _(i):
        pl.semaphore_signal(
            barrier, inc=1, device_id={"seq": lax.rem(me + i, SEQ)}, device_id_type=MESH
        )

    for t in (zp, yp, ym):
        pl.semaphore_signal(barrier, inc=1, device_id={"tensor": t}, device_id_type=MESH)

    @pl.loop(0, 8)
    def _(r):
        i = iota((64, 512), 0) + r * 64
        n = iota((64, 512), 1)
        same = ((i >> 7) == ((n >> 5) & 3)) & (((i >> 5) & 3) == (n >> 7)) & ((i & 31) == (n & 31))
        perm[pl.ds(pl.multiple_of(r * 64, 64), 64), :] = jnp.where(same, 1.0, 0.0).astype(BF16)

    def remote(src, dst, ss, rs, dev, axis="seq"):
        return pltpu.make_async_remote_copy(
            src_ref=src, dst_ref=dst, send_sem=ss, recv_sem=rs,
            device_id={axis: dev}, device_id_type=MESH,
        )

    def lanes(i):
        return pl.ds(pl.multiple_of(i * QUARTER, QUARTER), QUARTER)

    def deliver(dest, part, staged, landed, ss, rs):
        staged[dest] = part

        @pl.when(dest != me)
        def _():
            remote(staged.at[dest], landed.at[me], ss.at[dest], rs.at[me], dest).start()

        @pl.when(dest == me)
        def _():
            landed[me] = part

    def collect(landed, staged, ss, rs):
        @pl.loop(1, SEQ)
        def _(i):
            src = lax.rem(me + i, SEQ)
            remote(staged.at[src], landed.at[src], ss.at[src], rs.at[src], src).wait_recv()

    def settle(landed, staged, ss, rs):
        @pl.loop(1, SEQ)
        def _(i):
            src = lax.rem(me + i, SEQ)
            remote(staged.at[src], landed.at[src], ss.at[src], rs.at[src], src).wait_send()

    def node(dx, dz, other=False):
        c = 1 - core if other else core
        return lax.rem(x + dx, 4) * 8 + lax.rem(zh + dz, 4) * 2 + c

    sent = []

    def push(block, dev):
        index = len(sent)
        c = remote(wv.at[block], wv.at[block], wsend.at[index], wrecv.at[block], dev)
        sent.append(c)
        return c

    def pushed(block):
        remote(wv.at[block], wv.at[block], wsend.at[0], wrecv.at[block], node(0, 0, True)).wait_recv()

    def spread(dz):
        block = node(0, dz)
        for dev in (node(1, 0), node(3, 0), node(0, 0, True)):
            push(block, dev).start()

    def onward(dz):
        for dx in (3, 1):
            pushed(node(dx, dz))
            push(node(dx, dz), node(0, 0, True)).start()
        block = jnp.where(first_core, node(3, dz), node(1, dz))
        push(block, jnp.where(first_core, node(1, 0), node(3, 0))).start()

    loads[0].wait()
    pl.semaphore_wait(barrier, SEQ - 1 + 3)

    @pl.loop(0, OUTER)
    def _(i):
        tile = lax.rem(me // INNER + i, OUTER)
        parts = [kv[QUARTER * k : QUARTER * (k + 1), lanes(tile)] for k in range(INNER)]
        for q, part in enumerate(swap(parts, perm)):
            deliver(tile * INNER + q, part, xs, xr, xsend, xrecv)

    loads[2].wait()

    @pl.loop(0, OUTER)
    def _(i):
        tile = lax.rem(me // INNER + i, OUTER)
        parts = []
        for k in range(INNER):
            pair = [
                filt[pl.ds(m * 1024 + 256 * k + tile, UNIT, stride=8), :].astype(BF16)
                for m in range(2)
            ]
            parts.append(jnp.concatenate(pair, axis=0))
        for q, part in enumerate(swap(parts, perm)):
            deliver(tile * INNER + q, part, fs, fr, fsend, frecv)

    loads[1].wait()
    spread(0)

    group = iota((OUTER, 64), 0) == me // INNER
    listed = jnp.sum(jnp.where(group, blocks[...].astype(F32), 0.0), axis=0, keepdims=True)
    own = iota((KEPT, 64), 1) == (iota((KEPT, 64), 0) >> 1)
    column = jnp.sum(jnp.where(own, listed, 0.0), axis=1, keepdims=True)
    column = column.astype(jnp.int32) * 2 + (iota((KEPT, 1), 0) & 1)
    kcol[...] = jnp.broadcast_to(column, (KEPT, 128))
    own = iota((64, 64), 1) == iota((64, 64), 0)
    upright = jnp.sum(jnp.where(own, listed, 0.0), axis=1, keepdims=True)
    own = iota((64, KEPT), 0) == (iota((64, KEPT), 1) >> 1)
    row = jnp.sum(jnp.where(own, upright, 0.0), axis=0, keepdims=True)
    row = row.astype(jnp.int32) * 2 + (iota((1, KEPT), 1) & 1)
    krow[...] = jnp.broadcast_to(row, (8, KEPT))

    @pl.loop(0, KEPT // STEP)
    def _(r):
        rows = pl.ds(pl.multiple_of(r * STEP, STEP), STEP)
        more = pl.ds(pl.multiple_of(r * STEP + KEPT, STEP), STEP)
        phase = kcol[rows, 0:1] * iota((STEP, TOK), 1)
        ch, cl = halves(cosine_of(phase))
        sn = cosine_of(phase - 128)
        sh, sl = halves(sn)
        nh, nl = halves(-sn)
        mh[rows, 0:TOK] = ch
        ml[rows, 0:TOK] = cl
        mh[rows, TOK:] = sh
        ml[rows, TOK:] = sl
        mh[more, 0:TOK] = nh
        ml[more, 0:TOK] = nl
        mh[more, TOK:] = ch
        ml[more, TOK:] = cl

    @pl.loop(0, TOK // 64)
    def _(r):
        rows = pl.ds(pl.multiple_of(r * 64, 64), 64)
        more = pl.ds(pl.multiple_of(r * 64 + TOK, 64), 64)
        phase = krow[0:1, :] * (iota((64, KEPT), 0) + r * 64)
        ch, cl = halves(cosine_of(phase))
        sn = cosine_of(phase - 128)
        sh, sl = halves(sn)
        nh, nl = halves(-sn)
        th[rows, 0:KEPT] = ch
        tl[rows, 0:KEPT] = cl
        th[rows, KEPT:] = nh
        tl[rows, KEPT:] = nl
        th[more, 0:KEPT] = sh
        tl[more, 0:KEPT] = sl
        th[more, KEPT:] = ch
        tl[more, KEPT:] = cl

    @pl.loop(0, OUTER)
    def _(a):
        i, n = iota((128, 256), 0), iota((128, 256), 1)
        phase = ((i >> 5) * 8 + a) * ((n >> 5) & 3) + 8 * (n >> 7)
        hi, lo = halves(jnp.where((i & 31) == (n & 31), cosine_of(phase * 16), 0.0))
        dm[a, 0:128, :] = hi
        dm[a, 128:256, :] = lo
        n, i = iota((256, 128), 0), iota((256, 128), 1)
        phase = ((i >> 5) * 8 + a) * ((n >> 5) & 3) + 8 * (n >> 7)
        hi, lo = halves(jnp.where((i & 31) == (n & 31), cosine_of(phase * 16), 0.0))
        eh[a] = hi
        el[a] = lo

    @pl.loop(0, ROWS)
    def _(r):
        rows = pl.ds(pl.multiple_of(r * STEP, STEP), STEP)
        j = iota((STEP, 128), 0) + r * STEP
        alpha = (j * (iota((STEP, 128), 1) >> 5)).astype(F32) * (2 * math.pi / LENGTH)
        beta = (j * INNER).astype(F32) * (2 * math.pi / LENGTH)
        tw[0, rows, :] = sine(math.pi / 2 - alpha)
        tw[1, rows, :] = sine(alpha)
        tw[2, rows, :] = sine(math.pi / 2 - beta)
        tw[3, rows, :] = sine(beta)

    collect(xr, xs, xsend, xrecv)
    for dz in (1, 3):
        push(me, node(0, dz)).start()

    @pl.loop(0, OUTER)
    def _(a):
        for k, part in enumerate(swap([xr[OUTER * l + a] for l in range(INNER)], perm)):
            rq[QUARTER * k : QUARTER * (k + 1), 0:128] = part
            rq[QUARTER * k : QUARTER * (k + 1), 128:256] = part
        g[a] = dot(rq[...], dm[a])

    def twists(rows):
        tc, ts = tw[0, rows, :], tw[1, rows, :]
        uc, us = tw[2, rows, :], tw[3, rows, :]
        found = []
        for p in range(OUTER):
            found.append((tc, ts))
            if p + 1 < OUTER:
                tc, ts = tc * uc - ts * us, ts * uc + tc * us
        return found

    @pl.loop(0, ROWS)
    def _(r):
        rows = pl.ds(pl.multiple_of(r * STEP, STEP), STEP)
        more = pl.ds(pl.multiple_of(r * STEP + TOK, STEP), STEP)
        first = transform([(g[a, rows, 0:128], g[a, rows, 128:256]) for a in range(OUTER)], -1)
        for p, ((re, im), (tc, ts)) in enumerate(zip(first, twists(rows))):
            cols = slice(128 * (p % 2), 128 * (p % 2) + 128)
            fst[p // 2, rows, cols] = (re * tc + im * ts).astype(BF16)
            fst[p // 2, more, cols] = (im * tc - re * ts).astype(BF16)

    collect(fr, fs, fsend, frecv)
    @pl.loop(0, OUTER // 2)
    def _(w):
        for half in range(2):
            p = 2 * w + half
            cols = slice(128 * half, 128 * half + 128)
            for k, part in enumerate(swap([fr[INNER * p + l] for l in range(INNER)], perm)):
                fm[0, UNIT * k : UNIT * (k + 1), cols] = part[0:UNIT]
                fm[1, UNIT * k : UNIT * (k + 1), cols] = part[UNIT:]
        spectrum = dot(mh[...], fst[w]) + dot(ml[...], fst[w])
        sr, si = spectrum[0:KEPT], spectrum[KEPT:]
        f_re, f_im = fm[0].astype(F32), fm[1].astype(F32)
        product = jnp.concatenate([f_re * sr - f_im * si, f_re * si + f_im * sr], axis=0)
        hi, lo = halves(product)
        for part in range(2):
            rows = slice(TOK * part, TOK * (part + 1))
            g[2 * w + part] = dot(th[rows], hi) + dot(tl[rows], hi) + dot(th[rows], lo)

    for half in range(2):

        @pl.loop(half * (ROWS // 2), (half + 1) * (ROWS // 2))
        def _(r):
            rows = pl.ds(pl.multiple_of(r * STEP, STEP), STEP)
            turned = []
            for p, (tc, ts) in enumerate(twists(rows)):
                cols = slice(128 * (p % 2), 128 * (p % 2) + 128)
                re, im = g[p // 2 * 2, rows, cols], g[p // 2 * 2 + 1, rows, cols]
                turned.append(
                    (
                        (re * tc - im * ts).astype(BF16).astype(F32),
                        (re * ts + im * tc).astype(BF16).astype(F32),
                    )
                )
            for a, (re, im) in enumerate(transform(turned, 1)):
                hi, lo = halves(re)
                vh[a, rows, 0:128] = hi
                vl[a, rows, 0:128] = lo
                hi, lo = halves(im)
                vh[a, rows, 128:256] = hi
                vl[a, rows, 128:256] = lo

        @pl.loop(0, OUTER)
        def _(i):
            a = lax.rem(lax.rem(me, OUTER) + i, OUTER)
            rows = slice(HALF * half, HALF * (half + 1))
            v, rest = vh[a, rows], vl[a, rows]
            c = dot(v, eh[a]) + dot(rest, eh[a]) + dot(v, el[a])
            c = (c * (1.0 / LENGTH)).astype(BF16)
            parts = [c[64 * k : 64 * (k + 1)] for k in range(INNER)]
            for l, part in enumerate(swap(parts, perm)):
                deliver(
                    OUTER * l + a, part, cs.at[half], cr.at[half], csend.at[half], crecv.at[half]
                )

    loads[3].wait()

    for dz in (3, 1):
        pushed(node(0, dz))
        spread(dz)
    onward(0)
    hid = gath.at[ten]
    gathers = []
    ahead = jnp.where(first_core, yp, ym)

    def remote_rows(half, part, block, index, to):
        start, size = ((0, HALF), (0, UPPER), (UPPER, HALF - UPPER))[part]
        rows = pl.ds(HALF * half + start, size)
        return remote(
            gath.at[block, rows], gath.at[block, rows],
            gsend.at[index], grecv.at[part // 2, half, block], to, "tensor",
        )

    def gather(half, block, to, part=0):
        c = remote_rows(half, part, block, len(gathers), to)
        gathers.append(c)
        c.start()

    def arrived(half, block, part=0):
        remote_rows(half, part, block, 0, zp).wait_recv()

    def settled(half):
        collect(cr.at[half], cs.at[half], csend.at[half], crecv.at[half])

        @pl.loop(0, OUTER)
        def _(tile):
            parts = [cr[half, INNER * tile + q] for q in range(INNER)]
            for k, part in enumerate(swap(parts, perm)):
                rows = slice(HALF * half + 64 * k, HALF * half + 64 * (k + 1))
                direct = skip[0:1, lanes(tile)] * kv[rows, lanes(tile)].astype(F32)
                hid[rows, lanes(tile)] = (
                    gate[rows, lanes(tile)].astype(F32) * (part.astype(F32) + direct)
                ).astype(BF16)

        for to in (yp, ym, zp):
            gather(half, ten, to)

    def cross(half):
        arrived(half, zp)
        gather(half, zp, yp, 1)
        gather(half, zp, ym, 1)

    def ring(half):
        arrived(half, ym)
        arrived(half, yp)
        gather(half, jnp.where(first_core, ym, yp), ahead)
        gather(half, ym, zp, 2)
        gather(half, yp, zp, 2)

    def distant(half):
        arrived(half, far + down, 1)
        arrived(half, far + up, 1)
        gather(half, jnp.where(first_core, far + down, far + up), ahead, 1)

    def closing(half):
        arrived(half, near + across)
        gather(half, near + across, zp, 2)

    settled(0)
    push(
        jnp.where(first_core, node(0, 3), node(0, 1)),
        jnp.where(first_core, node(0, 1), node(0, 3)),
    ).start()
    settled(1)
    onward(3)
    onward(1)
    ring(0)
    cross(0)
    pushed(node(0, 2))
    spread(2)
    ring(1)
    cross(1)
    closing(0)
    distant(0)
    onward(2)
    closing(1)
    distant(1)
    for dz in (0, 3, 1, 2):
        pushed(node(2, dz))
        push(node(2, dz), node(0, 0, True)).start()
    for dx in range(4):
        for dz in range(4):
            pushed(node(dx, dz, True))

    def project(block, start=False):
        @pl.loop(0, 4)
        def _(n):
            cols = pl.ds(pl.multiple_of(n * 256, 256), 256)
            w = wv[pl.ds(INNER * block, INNER), :, cols].reshape(WIDTH, 256)
            part = dot(gath[block], w)
            acc[:, cols] = part if start else acc[:, cols] + part

    project(ten, True)
    project(zp)
    project(ym)
    project(yp)
    project(near + across)
    for block in (far + down, far + up):
        for half in range(2):
            arrived(half, block, 2)
        project(block)
    for half in range(2):
        arrived(half, far + across, 1)
        arrived(half, far + across, 2)
    project(far + across)
    out[...] = acc[...].astype(BF16)
    for c in gathers:
        c.wait_send()
    for c in sent:
        c.wait_send()
    settle(xr, xs, xsend, xrecv)
    settle(fr, fs, fsend, frecv)
    for half in range(2):
        settle(cr.at[half], cs.at[half], csend.at[half], crecv.at[half])


def body(keyval, gating, skip_gain, filter_values, blocks, out_weight):
    vmem = pl.BlockSpec(memory_space=pltpu.VMEM)
    away = pl.BlockSpec(memory_space=pl.ANY)
    dma = pltpu.SemaphoreType.DMA

    def buf(*shape, dtype=BF16):
        return pltpu.VMEM(shape, dtype)

    return pl.pallas_call(
        kernel,
        out_shape=jax.ShapeDtypeStruct((TOK, WIDTH), BF16),
        in_specs=[away, away, vmem, away, vmem, away],
        out_specs=vmem,
        scratch_shapes=[
            buf(KEPT, 128, dtype=jnp.int32), buf(8, KEPT, dtype=jnp.int32),
            buf(TOK, WIDTH), buf(TOK, WIDTH), buf(2048, 128, dtype=F32),
            buf(SEQ, 128, 128), buf(SEQ, 128, 128),
            buf(SEQ, 64, 128), buf(SEQ, 64, 128),
            buf(256, 1024), buf(256, 1024), buf(1024, 256), buf(1024, 256),
            buf(8, 256, 256), buf(8, 256, 128), buf(8, 256, 128), buf(512, 512),
            buf(4, 512, 128, dtype=F32), buf(512, 256), buf(8, 512, 256, dtype=F32),
            buf(4, 1024, 256), buf(2, 128, 256),
            buf(8, 512, 256), buf(8, 512, 256),
            buf(2, SEQ, 64, 128), buf(2, SEQ, 64, 128), buf(8, TOK, WIDTH),
            buf(SEQ, 256, WIDTH), buf(TOK, WIDTH, dtype=F32),
            dma((SEQ,)), dma((SEQ,)), dma((SEQ,)), dma((SEQ,)), dma((2, SEQ)), dma((2, SEQ)),
            dma((20,)), dma((2, 2, 8)), dma((31,)), dma((SEQ,)), dma((4,)),
        ],
        compiler_params=pltpu.CompilerParams(
            collective_id=0, has_side_effects=True, vmem_limit_bytes=60 * 2**20
        ),
    )(
        keyval, gating, skip_gain.reshape(1, WIDTH), filter_values.reshape(2048, 128),
        blocks, out_weight,
    )


def solution(mesh):
    placed = (
        P("seq", "tensor"),
        P("seq", "tensor"),
        P("tensor"),
        P(None, None, None, "seq", "tensor"),
        P("tensor", None),
        P("seq", "tensor"),
    )
    return jax.shard_map(
        body, mesh=mesh, in_specs=placed, out_specs=P("seq", "tensor"), check_vma=False
    )
```

```python
import math

import jax
import jax.numpy as jnp
from jax import lax
from jax.experimental import pallas as pl
from jax.experimental.pallas import tpu as pltpu
from jax.sharding import PartitionSpec as P

BLOCK = 64
SEQ = 32
OUTER = 8
INNER = 4
TOK = 512
QUARTER = 128
WIDTH = 1024
UNIT = 32
KEPT = 128
STEP = 16
ROWS = TOK // STEP
HALF = WIDTH // 2
UPPER = 448
WZ = 3
SEC = 2
RL = 1
E2 = 1
ORDER = "sawbxycdefzghivj"
LENGTH = SEQ * TOK
F32 = jnp.float32
BF16 = jnp.bfloat16
MESH = pl.DeviceIdType.MESH


def iota(shape, axis):
    return lax.broadcasted_iota(jnp.int32, shape, axis)


def sine(x):
    s = x * x
    t = -1.0 / 39916800.0
    for c in (1.0 / 362880.0, -1.0 / 5040.0, 1.0 / 120.0, -1.0 / 6.0, 1.0):
        t = t * s + c
    return x * t


def cosine_of(phase):
    d = jnp.abs((phase & 511) - 256) - 128
    return sine(d.astype(F32) * (math.pi / 256.0))


def halves(v):
    hi = v.astype(BF16)
    return hi, (v - hi.astype(F32)).astype(BF16)


def dot(a, b):
    return jnp.dot(a, b, preferred_element_type=F32)


def turn(v, num, den, sign):
    re, im = v
    num = num % den
    if num == 0:
        return v
    if 4 * num == den:
        return (-im, re) if sign > 0 else (im, -re)
    c = math.cos(2 * math.pi * num / den)
    s = sign * math.sin(2 * math.pi * num / den)
    if 8 * num == den:
        h = c
        return (h * (re - im), h * (re + im)) if sign > 0 else (h * (re + im), h * (im - re))
    if 8 * num == 3 * den:
        h = -c
        return (-h * (re + im), h * (re - im)) if sign > 0 else (h * (im - re), -h * (re + im))
    return (re * c - im * s, re * s + im * c)


def transform(values, sign):
    n = len(values)
    if n == 1:
        return values
    even = transform(values[0::2], sign)
    odd = transform(values[1::2], sign)
    odd = [turn(o, k, n, sign) for k, o in enumerate(odd)]
    low = [(e[0] + o[0], e[1] + o[1]) for e, o in zip(even, odd)]
    high = [(e[0] - o[0], e[1] - o[1]) for e, o in zip(even, odd)]
    return low + high


def swap(parts, perm):
    u = dot(jnp.concatenate(parts, axis=1), perm[...]).astype(BF16)
    return [u[:, QUARTER * i : QUARTER * (i + 1)] for i in range(INNER)]


def kernel(
    kv_in, gate_in, skip, filt_in, blocks, weight_in, out,
    kcol, krow, kv, gate, filt, xs, xr, fs, fr, mh, ml, th, tl, dm, eh, el, perm, tw, rq, g, fst, fm, vh, vl,
    cs, cr, gath, wv, acc,
    xsend, xrecv, fsend, frecv, csend, crecv, gsend, grecv, wsend, wrecv, local,
):
    me = lax.axis_index("seq")
    ten = lax.axis_index("tensor")
    zl, y = ten // 4, lax.rem(ten, 4)
    far, near = (1 - zl) * 4, zl * 4
    zp = far + y
    up, down, across = lax.rem(y + 1, 4), lax.rem(y + 3, 4), lax.rem(y + 2, 4)
    yp, ym = near + up, near + down
    core = lax.rem(me, 2)
    zh = lax.rem(me // 2, 4)
    x = me // 8
    first_core = core == 0

    loads = [
        pltpu.make_async_copy(kv_in, kv, local.at[0]),
        pltpu.make_async_copy(weight_in, wv.at[me], local.at[1]),
        pltpu.make_async_copy(filt_in, filt, local.at[2]),
        pltpu.make_async_copy(gate_in, gate, local.at[3]),
    ]
    for c in loads:
        c.start()

    barrier = pltpu.get_barrier_semaphore()

    @pl.loop(1, SEQ)
    def _(i):
        pl.semaphore_signal(
            barrier, inc=1, device_id={"seq": lax.rem(me + i, SEQ)}, device_id_type=MESH
        )

    for t in (zp, yp, ym):
        pl.semaphore_signal(barrier, inc=1, device_id={"tensor": t}, device_id_type=MESH)

    @pl.loop(0, 8)
    def _(r):
        i = iota((64, 512), 0) + r * 64
        n = iota((64, 512), 1)
        same = ((i >> 7) == ((n >> 5) & 3)) & (((i >> 5) & 3) == (n >> 7)) & ((i & 31) == (n & 31))
        perm[pl.ds(pl.multiple_of(r * 64, 64), 64), :] = jnp.where(same, 1.0, 0.0).astype(BF16)

    def remote(src, dst, ss, rs, dev, axis="seq"):
        return pltpu.make_async_remote_copy(
            src_ref=src, dst_ref=dst, send_sem=ss, recv_sem=rs,
            device_id={axis: dev}, device_id_type=MESH,
        )

    def lanes(i):
        return pl.ds(pl.multiple_of(i * QUARTER, QUARTER), QUARTER)

    def deliver(dest, part, staged, landed, ss, rs):
        staged[dest] = part

        @pl.when(dest != me)
        def _():
            remote(staged.at[dest], landed.at[me], ss.at[dest], rs.at[me], dest).start()

        @pl.when(dest == me)
        def _():
            landed[me] = part

    def collect(landed, staged, ss, rs):
        @pl.loop(1, SEQ)
        def _(i):
            src = lax.rem(me + i, SEQ)
            remote(staged.at[src], landed.at[src], ss.at[src], rs.at[src], src).wait_recv()

    def settle(landed, staged, ss, rs):
        @pl.loop(1, SEQ)
        def _(i):
            src = lax.rem(me + i, SEQ)
            remote(staged.at[src], landed.at[src], ss.at[src], rs.at[src], src).wait_send()

    def node(dx, dz, other=False):
        c = 1 - core if other else core
        return lax.rem(x + dx, 4) * 8 + lax.rem(zh + dz, 4) * 2 + c

    sent = []

    def push(block, dev):
        index = len(sent)
        c = remote(wv.at[block], wv.at[block], wsend.at[index], wrecv.at[block], dev)
        sent.append(c)
        return c

    def pushed(block):
        remote(wv.at[block], wv.at[block], wsend.at[0], wrecv.at[block], node(0, 0, True)).wait_recv()

    def spread(dz):
        block = node(0, dz)
        for dev in (node(1, 0), node(3, 0), node(0, 0, True)):
            push(block, dev).start()

    def onward(dz):
        for dx in (3, 1):
            pushed(node(dx, dz))
            push(node(dx, dz), node(0, 0, True)).start()
        block = jnp.where(first_core, node(3, dz), node(1, dz))
        push(block, jnp.where(first_core, node(1, 0), node(3, 0))).start()

    def begin():
        for dz in (1, 3):
            push(me, node(0, dz)).start()

    loads[0].wait()
    pl.semaphore_wait(barrier, SEQ - 1 + 3)

    for phase in range(2):

        @pl.loop(0, INNER)
        def _(i):
            plane = lax.rem(x + i, INNER)
            tile = INNER * phase + plane
            parts = [kv[QUARTER * k : QUARTER * (k + 1), lanes(tile)] for k in range(INNER)]
            for q, part in enumerate(swap(parts, perm)):
                deliver(plane * 8 + 2 * q + phase, part, xs, xr, xsend, xrecv)

        if phase == 0:
            loads[2].wait()

        @pl.loop(0, INNER)
        def _(i):
            plane = lax.rem(x + i, INNER)
            tile = INNER * phase + plane
            parts = []
            for k in range(INNER):
                pair = [
                    filt[pl.ds(m * 1024 + 256 * k + tile, UNIT, stride=8), :].astype(BF16)
                    for m in range(2)
                ]
                parts.append(jnp.concatenate(pair, axis=0))
            for q, part in enumerate(swap(parts, perm)):
                deliver(plane * 8 + 2 * q + phase, part, fs, fr, fsend, frecv)

    loads[1].wait()
    spread(0)
    if WZ == 3:
        begin()

    group = iota((OUTER, 64), 0) == INNER * core + x
    listed = jnp.sum(jnp.where(group, blocks[...].astype(F32), 0.0), axis=0, keepdims=True)
    own = iota((KEPT, 64), 1) == (iota((KEPT, 64), 0) >> 1)
    column = jnp.sum(jnp.where(own, listed, 0.0), axis=1, keepdims=True)
    column = column.astype(jnp.int32) * 2 + (iota((KEPT, 1), 0) & 1)
    kcol[...] = jnp.broadcast_to(column, (KEPT, 128))
    own = iota((64, 64), 1) == iota((64, 64), 0)
    upright = jnp.sum(jnp.where(own, listed, 0.0), axis=1, keepdims=True)
    own = iota((64, KEPT), 0) == (iota((64, KEPT), 1) >> 1)
    row = jnp.sum(jnp.where(own, upright, 0.0), axis=0, keepdims=True)
    row = row.astype(jnp.int32) * 2 + (iota((1, KEPT), 1) & 1)
    krow[...] = jnp.broadcast_to(row, (8, KEPT))

    @pl.loop(0, KEPT // STEP)
    def _(r):
        rows = pl.ds(pl.multiple_of(r * STEP, STEP), STEP)
        more = pl.ds(pl.multiple_of(r * STEP + KEPT, STEP), STEP)
        phase = kcol[rows, 0:1] * iota((STEP, TOK), 1)
        ch, cl = halves(cosine_of(phase))
        sn = cosine_of(phase - 128)
        sh, sl = halves(sn)
        nh, nl = halves(-sn)
        mh[rows, 0:TOK] = ch
        ml[rows, 0:TOK] = cl
        mh[rows, TOK:] = sh
        ml[rows, TOK:] = sl
        mh[more, 0:TOK] = nh
        ml[more, 0:TOK] = nl
        mh[more, TOK:] = ch
        ml[more, TOK:] = cl

    @pl.loop(0, TOK // 64)
    def _(r):
        rows = pl.ds(pl.multiple_of(r * 64, 64), 64)
        more = pl.ds(pl.multiple_of(r * 64 + TOK, 64), 64)
        phase = krow[0:1, :] * (iota((64, KEPT), 0) + r * 64)
        ch, cl = halves(cosine_of(phase))
        sn = cosine_of(phase - 128)
        sh, sl = halves(sn)
        nh, nl = halves(-sn)
        th[rows, 0:KEPT] = ch
        tl[rows, 0:KEPT] = cl
        th[rows, KEPT:] = nh
        tl[rows, KEPT:] = nl
        th[more, 0:KEPT] = sh
        tl[more, 0:KEPT] = sl
        th[more, KEPT:] = ch
        tl[more, KEPT:] = cl

    @pl.loop(0, OUTER)
    def _(a):
        i, n = iota((128, 256), 0), iota((128, 256), 1)
        phase = ((i >> 5) * 8 + a) * ((n >> 5) & 3) + 8 * (n >> 7)
        hi, lo = halves(jnp.where((i & 31) == (n & 31), cosine_of(phase * 16), 0.0))
        dm[a, 0:128, :] = hi
        dm[a, 128:256, :] = lo
        n, i = iota((256, 128), 0), iota((256, 128), 1)
        phase = ((i >> 5) * 8 + a) * ((n >> 5) & 3) + 8 * (n >> 7)
        hi, lo = halves(jnp.where((i & 31) == (n & 31), cosine_of(phase * 16), 0.0))
        eh[a] = hi
        el[a] = lo

    @pl.loop(0, ROWS)
    def _(r):
        rows = pl.ds(pl.multiple_of(r * STEP, STEP), STEP)
        j = iota((STEP, 128), 0) + r * STEP
        alpha = (j * (iota((STEP, 128), 1) >> 5)).astype(F32) * (2 * math.pi / LENGTH)
        beta = (j * INNER).astype(F32) * (2 * math.pi / LENGTH)
        tw[0, rows, :] = sine(math.pi / 2 - alpha)
        tw[1, rows, :] = sine(alpha)
        tw[2, rows, :] = sine(math.pi / 2 - beta)
        tw[3, rows, :] = sine(beta)

    collect(xr, xs, xsend, xrecv)
    if WZ == 2:
        begin()

    @pl.loop(0, OUTER)
    def _(a):
        for k, part in enumerate(swap([xr[OUTER * l + a] for l in range(INNER)], perm)):
            rq[QUARTER * k : QUARTER * (k + 1), 0:128] = part
            rq[QUARTER * k : QUARTER * (k + 1), 128:256] = part
        g[a] = dot(rq[...], dm[a])

    def twists(rows):
        tc, ts = tw[0, rows, :], tw[1, rows, :]
        uc, us = tw[2, rows, :], tw[3, rows, :]
        found = []
        for p in range(OUTER):
            found.append((tc, ts))
            if p + 1 < OUTER:
                tc, ts = tc * uc - ts * us, ts * uc + tc * us
        return found

    @pl.loop(0, ROWS)
    def _(r):
        rows = pl.ds(pl.multiple_of(r * STEP, STEP), STEP)
        more = pl.ds(pl.multiple_of(r * STEP + TOK, STEP), STEP)
        first = transform([(g[a, rows, 0:128], g[a, rows, 128:256]) for a in range(OUTER)], -1)
        for p, ((re, im), (tc, ts)) in enumerate(zip(first, twists(rows))):
            cols = slice(128 * (p % 2), 128 * (p % 2) + 128)
            fst[p // 2, rows, cols] = (re * tc + im * ts).astype(BF16)
            fst[p // 2, more, cols] = (im * tc - re * ts).astype(BF16)

    collect(fr, fs, fsend, frecv)
    @pl.loop(0, OUTER // 2)
    def _(w):
        for half in range(2):
            p = 2 * w + half
            cols = slice(128 * half, 128 * half + 128)
            for k, part in enumerate(swap([fr[INNER * p + l] for l in range(INNER)], perm)):
                fm[0, UNIT * k : UNIT * (k + 1), cols] = part[0:UNIT]
                fm[1, UNIT * k : UNIT * (k + 1), cols] = part[UNIT:]
        spectrum = dot(mh[...], fst[w]) + dot(ml[...], fst[w])
        sr, si = spectrum[0:KEPT], spectrum[KEPT:]
        f_re, f_im = fm[0].astype(F32), fm[1].astype(F32)
        product = jnp.concatenate([f_re * sr - f_im * si, f_re * si + f_im * sr], axis=0)
        hi, lo = halves(product)
        for part in range(2):
            rows = slice(TOK * part, TOK * (part + 1))
            g[2 * w + part] = dot(th[rows], hi) + dot(tl[rows], hi) + dot(th[rows], lo)

    @pl.loop(0, ROWS)
    def _(r):
        rows = pl.ds(pl.multiple_of(r * STEP, STEP), STEP)
        turned = []
        for p, (tc, ts) in enumerate(twists(rows)):
            cols = slice(128 * (p % 2), 128 * (p % 2) + 128)
            re, im = g[p // 2 * 2, rows, cols], g[p // 2 * 2 + 1, rows, cols]
            turned.append(
                (
                    (re * tc - im * ts).astype(BF16).astype(F32),
                    (re * ts + im * tc).astype(BF16).astype(F32),
                )
            )
        for a, (re, im) in enumerate(transform(turned, 1)):
            hi, lo = halves(re)
            vh[a, rows, 0:128] = hi
            vl[a, rows, 0:128] = lo
            hi, lo = halves(im)
            vh[a, rows, 128:256] = hi
            vl[a, rows, 128:256] = lo

    @pl.loop(0, OUTER)
    def _(i):
        a = lax.rem(lax.rem(me, OUTER) + i, OUTER)
        c = dot(vh[a], eh[a]) + dot(vl[a], eh[a]) + dot(vh[a], el[a])
        c = (c * (1.0 / LENGTH)).astype(BF16)
        parts = [c[QUARTER * k : QUARTER * (k + 1)] for k in range(INNER)]
        for l, part in enumerate(swap(parts, perm)):
            deliver(OUTER * l + a, part, cs, cr, csend, crecv)

    if WZ == 0:
        begin()
    loads[3].wait()

    gathers = []
    ahead = jnp.where(first_core, yp, ym)

    def remote_rows(half, part, block, index, to):
        start, size = ((0, TOK), (0, UPPER), (UPPER, TOK - UPPER))[part]
        rows = pl.ds(start, size)
        return remote(
            gath.at[block, half, rows], gath.at[block, half, rows],
            gsend.at[index], grecv.at[part // 2, half, block], to, "tensor",
        )

    def gather(half, block, to, part=0):
        c = remote_rows(half, part, block, len(gathers), to)
        gathers.append(c)
        c.start()

    def arrived(half, block, part=0):
        remote_rows(half, part, block, 0, zp).wait_recv()

    def settled(half):
        @pl.loop(0, SEQ // 2)
        def _(i):
            src = 2 * i + half

            @pl.when(src != me)
            def _():
                remote(cs.at[src], cr.at[src], csend.at[src], crecv.at[src], src).wait_recv()

        @pl.loop(0, INNER)
        def _(plane):
            tile = INNER * half + plane
            parts = [cr[plane * 8 + 2 * q + half] for q in range(INNER)]
            for k, part in enumerate(swap(parts, perm)):
                rows = slice(QUARTER * k, QUARTER * (k + 1))
                direct = skip[0:1, lanes(tile)] * kv[rows, lanes(tile)].astype(F32)
                gath[ten, half, rows, lanes(plane)] = (
                    gate[rows, lanes(tile)].astype(F32) * (part.astype(F32) + direct)
                ).astype(BF16)

        for to in (yp, ym, zp):
            gather(half, ten, to)

    def cross(half):
        arrived(half, zp)
        gather(half, zp, yp, 1)
        gather(half, zp, ym, 1)

    def ring(half):
        arrived(half, ym)
        arrived(half, yp)
        gather(half, jnp.where(first_core, ym, yp), ahead)
        gather(half, ym, zp, 2)
        gather(half, yp, zp, 2)

    def distant(half):
        arrived(half, far + down, 1)
        arrived(half, far + up, 1)
        gather(half, jnp.where(first_core, far + down, far + up), ahead, 1)

    def closing(half):
        arrived(half, near + across)
        gather(half, near + across, zp, 2)

    def forward():
        push(
            jnp.where(first_core, node(0, 3), node(0, 1)),
            jnp.where(first_core, node(0, 1), node(0, 3)),
        ).start()

    def second():
        for dz in (3, 1):
            pushed(node(0, dz))
            spread(dz)
        if RL == 1:
            forward()
        onward(0)

    def early():
        pushed(node(0, 2))
        spread(2)

    def last():
        for dz in (0, 3, 1, 2):
            pushed(node(2, dz))
            push(node(2, dz), node(0, 0, True)).start()

    steps = dict(
        a=lambda: settled(0), b=lambda: settled(1), c=lambda: ring(0), d=lambda: cross(0),
        e=lambda: ring(1), f=lambda: cross(1), g=lambda: closing(0), h=lambda: distant(0),
        i=lambda: closing(1), j=lambda: distant(1), w=lambda: early(), x=lambda: onward(3),
        y=lambda: onward(1), z=lambda: onward(2), v=lambda: last(), s=lambda: second(),
    )
    for key in ORDER:
        steps[key]()

    for dx in range(4):
        for dz in range(4):
            pushed(node(dx, dz, True))

    def project(block, start=False):
        @pl.loop(0, 4)
        def _(n):
            cols = pl.ds(pl.multiple_of(n * 256, 256), 256)
            low = wv[pl.ds(INNER * block, 2), :, cols].reshape(HALF, 256)
            high = wv[pl.ds(INNER * block + 2, 2), :, cols].reshape(HALF, 256)
            part = dot(gath[block, 0], low) + dot(gath[block, 1], high)
            acc[:, cols] = part if start else acc[:, cols] + part

    project(ten, True)
    project(zp)
    project(ym)
    project(yp)
    project(near + across)
    for block in (far + down, far + up):
        for half in range(2):
            arrived(half, block, 2)
        project(block)
    for half in range(2):
        arrived(half, far + across, 1)
        arrived(half, far + across, 2)
    project(far + across)
    out[...] = acc[...].astype(BF16)
    for c in gathers:
        c.wait_send()
    for c in sent:
        c.wait_send()
    settle(xr, xs, xsend, xrecv)
    settle(fr, fs, fsend, frecv)
    settle(cr, cs, csend, crecv)


def body(keyval, gating, skip_gain, filter_values, blocks, out_weight):
    vmem = pl.BlockSpec(memory_space=pltpu.VMEM)
    away = pl.BlockSpec(memory_space=pl.ANY)
    dma = pltpu.SemaphoreType.DMA

    def buf(*shape, dtype=BF16):
        return pltpu.VMEM(shape, dtype)

    return pl.pallas_call(
        kernel,
        out_shape=jax.ShapeDtypeStruct((TOK, WIDTH), BF16),
        in_specs=[away, away, vmem, away, vmem, away],
        out_specs=vmem,
        scratch_shapes=[
            buf(KEPT, 128, dtype=jnp.int32), buf(8, KEPT, dtype=jnp.int32),
            buf(TOK, WIDTH), buf(TOK, WIDTH), buf(2048, 128, dtype=F32),
            buf(SEQ, 128, 128), buf(SEQ, 128, 128),
            buf(SEQ, 64, 128), buf(SEQ, 64, 128),
            buf(256, 1024), buf(256, 1024), buf(1024, 256), buf(1024, 256),
            buf(8, 256, 256), buf(8, 256, 128), buf(8, 256, 128), buf(512, 512),
            buf(4, 512, 128, dtype=F32), buf(512, 256), buf(8, 512, 256, dtype=F32),
            buf(4, 1024, 256), buf(2, 128, 256),
            buf(8, 512, 256), buf(8, 512, 256),
            buf(SEQ, 128, 128), buf(SEQ, 128, 128), buf(8, 2, TOK, HALF),
            buf(SEQ, 256, WIDTH), buf(TOK, WIDTH, dtype=F32),
            dma((SEQ,)), dma((SEQ,)), dma((SEQ,)), dma((SEQ,)), dma((SEQ,)), dma((SEQ,)),
            dma((20,)), dma((2, 2, 8)), dma((31,)), dma((SEQ,)), dma((4,)),
        ],
        compiler_params=pltpu.CompilerParams(
            collective_id=0, has_side_effects=True, vmem_limit_bytes=60 * 2**20
        ),
    )(
        keyval, gating, skip_gain.reshape(1, WIDTH), filter_values.reshape(2048, 128),
        blocks, out_weight,
    )


def solution(mesh):
    placed = (
        P("seq", "tensor"),
        P("seq", "tensor"),
        P("tensor"),
        P(None, None, None, "seq", "tensor"),
        P("tensor", None),
        P("seq", "tensor"),
    )
    return jax.shard_map(
        body, mesh=mesh, in_specs=placed, out_specs=P("seq", "tensor"), check_vma=False
    )
```
